256 devices in a mesh: dp: 8 (over z_hi, y), seq: 32 (over x, z_lo, core).
Axes of the slice: x: 4, y: 4, z: 8 (z_hi: 2, z_lo: 4; z = z_hi * 4 + z_lo), core: 2. Of those that a mesh axis runs over, the one named last changes fastest.
Arguments:
- patches: bfloat16 [8, 4096, 2048], P('dp', 'seq'), may hold values from -6 to 6
- key_proj: bfloat16 [8, 4096, 128], P('dp', 'seq'), may hold values from -6 to 6
- query_proj: bfloat16 [8, 4096, 128], P('dp', 'seq'), may hold values from -6 to 6
- step_raw: float32 [8, 32, 4096], P('dp', None, 'seq'), may hold values from -16 to -1
- log_decay: float32 [2, 32], replicated, may hold values from -0.7 to 0.7
- step_bias: float32 [2, 32], replicated, may hold values from -0.5 to 0.5
- skip_gain: float32 [32], replicated, may hold values from 0.5 to 1.5
- group_valid: int32 [8, 32], P('dp', 'seq'), may hold values 0 or 1
- out_grad: bfloat16 [8, 4096, 2048], P('dp', 'seq'), may hold values from -6 to 6
Outputs:
- output: bfloat16 [8, 4096, 2048], P('dp', 'seq')
- patch_grad: bfloat16 [8, 4096, 2048], P('dp', 'seq')
- key_grad: float32 [8, 4096, 128], P('dp', 'seq')
- query_grad: float32 [8, 4096, 128], P('dp', 'seq')
- step_grad: float32 [8, 32, 4096], P('dp', None, 'seq')
- decay_grad: float32 [2, 32], replicated
- bias_grad: float32 [2, 32], replicated
- skip_grad: float32 [32], replicated
The draws below stay inside these ranges and needn't reach their ends.
All inputs are finite; a program needn't handle non-finite values. No bound on the sum of `group_valid` on one device may be relied on, other than what follows from the above.
Results may differ from the reference program's by a relative error of at most 0.0037.
Values may be sent and summed in bfloat16 or wider, within the bound.
A program may use at most 320 MiB of HBM per device.

```python
import math
from functools import partial
import jax
import jax.numpy as jnp
from jax import lax

LOCAL_HEADS = 32
STATE = 128
GROUP = 128
TOK_DEV = 128
WIDTH = 2048
SAMPLE_BATCH = 8
SEQUENCE_LENGTH = 4096


def draw_step_raw(key, part):
    random_subkeys = jax.random.split(key, 5)
    exponent = 2.0
    lowest = math.log(0.5 / SEQUENCE_LENGTH)
    upper_level = math.log(0.04)
    fraction = jax.random.uniform(random_subkeys[0], (SAMPLE_BATCH, LOCAL_HEADS, 1), dtype=jnp.float32)
    baseline = lowest + (upper_level - lowest) * fraction ** exponent
    roughness = jax.random.uniform(random_subkeys[1], (SAMPLE_BATCH, LOCAL_HEADS, SEQUENCE_LENGTH), dtype=jnp.float32, minval=-0.7, maxval=0.7)
    device_shift = jnp.repeat(jax.random.uniform(random_subkeys[2], (SAMPLE_BATCH, 1, SEQUENCE_LENGTH // TOK_DEV), dtype=jnp.float32, minval=-0.5, maxval=0.5), TOK_DEV, axis=2)
    level_values = baseline + roughness + device_shift
    spike_positions = jax.random.randint(random_subkeys[3], (SAMPLE_BATCH, 1, 3), 0, SEQUENCE_LENGTH)
    spike_hit = jnp.any(jnp.arange(SEQUENCE_LENGTH)[None, None, :, None] == spike_positions[:, :, None, :], axis=3)
    spike_level = jax.random.uniform(random_subkeys[4], (SAMPLE_BATCH, LOCAL_HEADS, SEQUENCE_LENGTH), dtype=jnp.float32, minval=-1.8, maxval=-1.2)
    return jnp.where(spike_hit, spike_level, level_values).astype(jnp.float32)


def touch_ends(values, rng, least, top_value):
    place = [jax.random.randint(jax.random.fold_in(rng, axis), (), 0, length) for axis, length in enumerate(values.shape)]
    main_axis = values.shape.index(max(values.shape))
    neighbour = place[:main_axis] + [(place[main_axis] + 1) % values.shape[main_axis]] + place[main_axis + 1:]
    return values.at[tuple(place)].set(least).at[tuple(neighbour)].set(top_value)


def levels(stream_key, shape, cuts, smallest, largest):
    level = 1.0
    for axis_at, shards_of in cuts:
        steps = jax.random.uniform(jax.random.fold_in(jax.random.fold_in(stream_key, 6), axis_at), (shards_of,), jnp.float32, smallest / len(cuts), largest / len(cuts))
        level = level * jnp.repeat(jnp.exp(steps), shape[axis_at] // shards_of).reshape((-1,) + (1,) * (len(shape) - 1 - axis_at))
    return level


def bell_draw(own_key, shape, scale, most, cuts=(), held_as=jnp.bfloat16):
    values = scale * jax.random.normal(own_key, shape, jnp.float32)
    if cuts:
        values = values * levels(own_key, shape, cuts, -0.22, 0.18)
    return jnp.clip(values, -most, most).astype(held_as)


def setup_inputs(seed: int = 0) -> dict:
    seeds = jax.random.split(jax.random.key(seed), 10)
    return {
        "patches": bell_draw(seeds[0], (SAMPLE_BATCH, SEQUENCE_LENGTH, WIDTH), 1.0, 6.0, ((0, 8), (1, 32))),
        "key_proj": bell_draw(seeds[1], (SAMPLE_BATCH, SEQUENCE_LENGTH, STATE), 1.0, 6.0, ((0, 8), (1, 32))),
        "query_proj": bell_draw(seeds[2], (SAMPLE_BATCH, SEQUENCE_LENGTH, STATE), 1.0, 6.0, ((0, 8), (1, 32))),
        "step_raw": draw_step_raw(jax.random.fold_in(seeds[9], 71), 0),
        "log_decay": jnp.clip(jax.random.uniform(seeds[4], (2, LOCAL_HEADS), jnp.float32, -0.7, 0.7), -0.7, 0.7),
        "step_bias": jnp.clip(jax.random.uniform(seeds[5], (2, LOCAL_HEADS), jnp.float32, -0.5, 0.5), -0.5, 0.5),
        "skip_gain": jnp.clip(jax.random.uniform(seeds[6], (LOCAL_HEADS,), jnp.float32, 0.5, 1.5), 0.5, 1.5),
        "group_valid": touch_ends((jax.random.randint(seeds[7], (SAMPLE_BATCH, SEQUENCE_LENGTH // GROUP), 0, 8) < 7).astype(jnp.int32), jax.random.fold_in(seeds[7], 1), 0, 1),
        "out_grad": bell_draw(seeds[8], (SAMPLE_BATCH, SEQUENCE_LENGTH, WIDTH), 1.0, 6.0, ((0, 8), (1, 32))),
    }


highest = lax.Precision.HIGHEST

def cumulative_decay(step_rows, decay_rate):
    return jnp.cumsum(step_rows * decay_rate[None, :, None], axis=2)

def group_states(inputs, key_rows, step_rows, decay_rate):
    cumulative = cumulative_decay(step_rows, decay_rate)
    to_end = jnp.exp(cumulative[:, :, -1:] - cumulative) * step_rows
    weighted = inputs * jnp.transpose(to_end, (0, 2, 1))[:, :, :, None]
    states = jnp.einsum('kqhp,kqn->khpn', weighted, key_rows, precision=highest)
    return (cumulative[:, :, -1], states)

def run_groups(log_group, states, start_state):

    def advance(running, pieces):
        log_piece, state_piece = pieces
        return (jnp.exp(log_piece)[:, None, None] * running + state_piece, running)
    final_state, entering = lax.scan(advance, start_state, (log_group, states))
    return (entering, final_state)

def enter_states(log_group, states, start_state):
    return run_groups(log_group, states, start_state)[0]

def group_outputs(inputs, key_rows, query_rows, step_rows, decay_rate, entering):
    cumulative = cumulative_decay(step_rows, decay_rate)
    length = cumulative.shape[2]
    causal = jnp.arange(length)[:, None] >= jnp.arange(length)[None, :]
    spread = cumulative[:, :, :, None] - cumulative[:, :, None, :]
    within = jnp.where(causal, jnp.exp(jnp.where(causal, spread, 0.0)), 0.0)
    scores = jnp.einsum('kqn,ksn->kqs', query_rows, key_rows, precision=highest)
    mixing = within * scores[:, None, :, :]
    driven = inputs * jnp.transpose(step_rows, (0, 2, 1))[:, :, :, None]
    inside = jnp.einsum('khqs,kshp->kqhp', mixing, driven, precision=highest)
    carried = jnp.einsum('kqn,khpn->kqhp', query_rows, entering, precision=highest)
    return inside + carried * jnp.transpose(jnp.exp(cumulative), (0, 2, 1))[:, :, :, None]

def direction(patch_rows, key_rows, query_rows, raw_steps, bias_row, decay_row, token_mask):
    rows_total, feat_width = patch_rows.shape
    head_count = raw_steps.shape[0]
    block_count = rows_total // GROUP
    inputs = patch_rows.reshape(block_count, GROUP, head_count, feat_width // head_count)
    keyed = key_rows.reshape(block_count, GROUP, -1)
    queried = query_rows.reshape(block_count, GROUP, -1)
    step_rows = (jax.nn.softplus(raw_steps + bias_row[:, None]) * token_mask[None, :]).reshape(head_count, block_count, GROUP).transpose(1, 0, 2)
    decay_rate = -jnp.exp(decay_row)
    log_group, states = group_states(inputs, keyed, step_rows, decay_rate)
    entering = enter_states(log_group, states, jnp.zeros_like(states[0]))
    return group_outputs(inputs, keyed, queried, step_rows, decay_rate, entering).reshape(rows_total, feat_width)

def reference(patches, key_proj, query_proj, step_raw, log_decay, step_bias, skip_gain, group_valid, out_grad):
    head_count = step_raw.shape[1]

    def one_sample(pieces):
        patch_row, key_row, query_row, step_row, valid_row, grad_row = pieces
        token_mask = jnp.repeat(valid_row.astype(jnp.float32), GROUP)
        patch_wide = patch_row.astype(jnp.float32)
        key_wide = key_row.astype(jnp.float32)
        query_wide = query_row.astype(jnp.float32)
        rows_total, feat_width = patch_wide.shape
        head_dim = feat_width // head_count
        cotangent = grad_row.astype(jnp.float32) * token_mask[:, None]
        fwd_out, fwd_back = jax.vjp(partial(direction, token_mask=token_mask), patch_wide, key_wide, query_wide, step_row, step_bias[0], log_decay[0])
        grads_fwd = fwd_back(cotangent)
        rev_out, rev_back = jax.vjp(partial(direction, token_mask=token_mask[::-1]), patch_wide[::-1], key_wide[::-1], query_wide[::-1], step_row[:, ::-1], step_bias[1], log_decay[1])
        grads_rev = rev_back(cotangent[::-1])
        rev_rounded = lax.optimization_barrier(rev_out[::-1].astype(jnp.bfloat16)).astype(jnp.float32)
        skip_wide = jnp.repeat(skip_gain, head_dim)
        output = (token_mask[:, None] * (fwd_out + rev_rounded + skip_wide[None, :] * patch_wide)).astype(jnp.bfloat16)
        rev_patch = lax.optimization_barrier(grads_rev[0][::-1].astype(jnp.bfloat16)).astype(jnp.float32)
        patch_grad = (grads_fwd[0] + rev_patch + skip_wide[None, :] * cotangent).astype(jnp.bfloat16)
        key_grad = grads_fwd[1] + grads_rev[1][::-1]
        query_grad = grads_fwd[2] + grads_rev[2][::-1]
        step_grad = grads_fwd[3] + grads_rev[3][:, ::-1]
        bias_grad = jnp.stack([grads_fwd[4], grads_rev[4]])
        decay_grad = jnp.stack([grads_fwd[5], grads_rev[5]])
        skip_grad = lax.optimization_barrier(jnp.sum((cotangent * patch_wide).reshape(rows_total, head_count, head_dim), axis=(0, 2)))
        return (output, patch_grad, key_grad, query_grad, step_grad, decay_grad, bias_grad, skip_grad)
    results = lax.map(one_sample, (patches, key_proj, query_proj, step_raw, group_valid, out_grad))
    return (results[0], results[1], results[2], results[3], results[4], lax.optimization_barrier(jnp.sum(results[5], axis=0)), lax.optimization_barrier(jnp.sum(results[6], axis=0)), lax.optimization_barrier(jnp.sum(results[7], axis=0)))
```

```python
import functools

import jax
import jax.numpy as jnp
from jax import lax
from jax.experimental import pallas as pl
from jax.experimental.pallas import tpu as pltpu
from jax.sharding import PartitionSpec as P

F32 = jnp.float32
BF16 = jnp.bfloat16
MESH = pl.DeviceIdType.MESH
TOK = 128
LANES = 128
HIGH = lax.Precision.HIGHEST

SCAN_DIR = (0, 1, 1, 0)
SCAN_LEFT = (False, False, True, True)


def dot(a, b, dims=((1,), (0,)), precision=None):
    return lax.dot_general(
        a, b, (dims, ((), ())), precision=precision, preferred_element_type=F32
    )


def iota(shape, axis):
    return lax.broadcasted_iota(jnp.int32, shape, axis)


def split2(v):
    hi = v.astype(BF16)
    return hi, (v - hi.astype(F32)).astype(BF16)


def split3(v):
    hi = v.astype(BF16)
    rest = v - hi.astype(F32)
    mid = rest.astype(BF16)
    return hi, mid, (rest - mid.astype(F32)).astype(BF16)


def column(row):
    heads = row.shape[1]
    eye = iota((heads, heads), 0) == iota((heads, heads), 1)
    return jnp.sum(jnp.where(eye, jnp.broadcast_to(row, (heads, heads)), 0.0), axis=1, keepdims=True)


def softplus(v):
    z = jnp.exp(-jnp.abs(v))
    u = z / (2.0 + z)
    q = u * u
    series = 1.0 / 17.0
    for term in (15.0, 13.0, 11.0, 9.0, 7.0, 5.0, 3.0, 1.0):
        series = series * q + 1.0 / term
    return jnp.maximum(v, 0.0) + 2.0 * u * series


def timing(raw, log_decay, step_bias, mask, r):
    rate = -jnp.exp(column(log_decay[r : r + 1, :]))
    shifted = raw + column(step_bias[r : r + 1, :])
    soft = softplus(shifted)
    slope = 1.0 / (1.0 + jnp.exp(-shifted))
    steps = soft * mask
    logs = steps * rate
    upto = (iota((TOK, TOK), 0) <= iota((TOK, TOK), 1)).astype(F32)
    cum = dot(logs, upto, precision=HIGH)
    total = cum[:, TOK - 1 :]
    if r == 0:
        place = cum
        weight = jnp.exp(total - cum) * steps
        decay = jnp.exp(cum)
    else:
        place = cum - logs
        weight = jnp.exp(place) * steps
        decay = jnp.exp(total - place)
    return dict(
        rate=rate, soft=soft, slope=slope, steps=steps, total=total, place=place,
        weight=weight, decay=decay,
    )


def spread(pair, tile):
    rows = pair.shape[0]
    heads = rows // 2
    pick = iota((rows, LANES), 0)
    pick = jnp.where(pick >= heads, pick - heads, pick)
    mine = 2 * tile + (iota((rows, LANES), 1) >= LANES // 2).astype(jnp.int32)
    sel = jnp.where(pick == mine, 1.0, 0.0).astype(BF16)
    return dot(pair, sel, ((0,), (0,)))


def two_parts(v):
    hi, lo = split2(v)
    return jnp.concatenate([hi.astype(F32), lo.astype(F32)], axis=0).astype(BF16)


UNROLL = 2
PLAN = (5, 4, 4, 2, 1)
LINK = (BF16, BF16, BF16, F32, F32)


def pair_rows(v):
    hi, lo = split2(v)
    return jnp.concatenate([hi, lo], axis=0)


def pair_lanes(v):
    hi, lo = split2(v)
    return jnp.concatenate([hi, lo], axis=1)


def layer_kernel(
    x_ref, g_ref, key_ref, query_ref, raw_ref, ld_ref, sb_ref, skip_ref, valid_ref,
    out_ref, pg_ref, kg_ref, qg_ref, sg_ref, dec_ref, bias_ref, skipg_ref,
    seg, seg_in, coef, own, got, snd, eown, egot, esnd, e_hi, e_lo,
    y_ref, dx_ref, ge_ref, ds_ref, dk_ref, dq_ref, sums_ref, part_a, part_b, part_c,
    up_send, up_recv, down_send, down_recv, log_send, log_recv,
    sum_send, sum_recv, *, levels, units, tiles, line, rows_of, groups
):
    me = lax.axis_index("seq")
    my_dp = lax.axis_index("dp")
    bits = [(me // (1 << b)) % 2 for b in range(levels)]
    peers = [me + (1 << b) * (1 - 2 * bits[b]) for b in range(levels)]
    half = [units >> (b + 1) for b in range(levels)]
    base = [0]
    for b in range(levels):
        base.append(base[b] + bits[b] * half[b])

    in_line = me % line
    my_line = me // line
    sum_peers = (
        [{"seq": my_line * line + (in_line + k) % line} for k in range(1, line)],
        [{"seq": (my_line + k) % rows_of * line + in_line} for k in range(1, rows_of)],
        [{"dp": (my_dp + k) % groups} for k in range(1, groups)],
    )
    sum_place = (in_line, my_line, my_dp)
    sum_size = (line, rows_of, groups)

    barrier = pltpu.get_barrier_semaphore()
    greeted = 0
    for group in sum_peers:
        for device in group:
            pl.semaphore_signal(barrier, inc=1, device_id=device, device_id_type=MESH)
            greeted += 1

    mask = valid_ref[0, 0].astype(F32)
    raw = raw_ref[...]
    logd = ld_ref[...]
    bias = sb_ref[...]
    heads = raw.shape[0]
    t = [timing(raw, logd, bias, mask, r) for r in (0, 1)]
    pick = iota((tiles, heads), 1)
    even = (pick == 2 * iota((tiles, heads), 0)).astype(F32)
    odd = (pick == 2 * iota((tiles, heads), 0) + 1).astype(F32)
    left_row = iota((tiles, LANES), 1) < LANES // 2
    for r in (0, 1):
        wide = jnp.broadcast_to(t[r]["total"], (heads, LANES))
        seg[0, r] = jnp.where(
            left_row, dot(even, wide, precision=HIGH), dot(odd, wide, precision=HIGH)
        )
    w = [two_parts(t[r]["weight"]) for r in (0, 1)]
    e = [two_parts(t[r]["decay"]) for r in (0, 1)]
    key = key_ref[...]
    query = query_ref[...]

    pl.semaphore_wait(barrier, greeted)

    def push(src, dst, send, recv, b):
        return pltpu.make_async_remote_copy(
            src_ref=src, dst_ref=dst, send_sem=send, recv_sem=recv,
            device_id={"seq": peers[b]}, device_id_type=MESH,
        )

    def up_copy(b, a):
        return push(snd[b].at[a], got[b].at[a], up_send.at[b, a], up_recv.at[b, a], b)

    def down_copy(b, a):
        if b == 0:
            dst = e_hi.at[a, pl.ds(bits[0] * half[0], half[0])]
        else:
            dst = egot[b].at[a]
        return push(esnd[b].at[a], dst, down_send.at[b, a], down_recv.at[b, a], b)

    def log_copy(b):
        return push(seg.at[b], seg_in.at[b], log_send.at[b], log_recv.at[b], b)

    def late_flag(b, a):
        late = (1 - bits[b]) if SCAN_LEFT[a] else bits[b]
        return late.astype(F32)

    def factors(b):
        log_copy(b).wait_recv()
        mine, other = seg[b], seg_in[b]
        if b + 1 < levels:
            seg[b + 1] = mine + other
            log_copy(b + 1).start()
        for a in range(4):
            r = SCAN_DIR[a]
            late = late_flag(b, a)
            coef[b, a, 0] = jnp.exp((1.0 - late) * other[r])
            coef[b, a, 1] = jnp.exp(late * mine[r])
            coef[b, a, 2] = jnp.exp(late * other[r])
            coef[b, a, 3] = jnp.exp((1.0 - late) * mine[r])

    log_copy(0).start()

    key_t = key.astype(F32).T.astype(BF16)
    query_t = query.astype(F32).T.astype(BF16)
    key_tt = jnp.concatenate([key_t, key_t], axis=1)
    query_tt = jnp.concatenate([query_t, query_t], axis=1)
    half_tiles = tiles // 2
    scale = (w[0], e[1], w[1], e[0])
    for a in range(4):
        is_state = a % 2 == 0
        ref, lhs = (x_ref, key_tt) if is_state else (g_ref, query_tt)

        def state(j, ref=ref, lhs=lhs, a=a, is_state=is_state):
            lanes = pl.ds(pl.multiple_of(j * LANES, LANES), LANES)
            v = ref[:, lanes].astype(F32) * spread(scale[a], j)
            if not is_state:
                v = v * mask
            return dot(lhs, pair_rows(v)).reshape(2, TOK // 2, LANES)

        def state_out(i, carry, a=a, state=state):
            u = state((1 - bits[0]) * half_tiles + i)
            snd[0][a, pl.ds(2 * i, 2)] = u.astype(snd[0].dtype)
            return carry

        def state_keep(i, carry, a=a, state=state):
            own[0][a, pl.ds(2 * i, 2)] = state(bits[0] * half_tiles + i)
            return carry

        lax.fori_loop(0, half_tiles, state_out, 0, unroll=UNROLL)
        up_copy(0, a).start()
        lax.fori_loop(0, half_tiles, state_keep, 0, unroll=UNROLL)
        if a < levels:
            factors(a)
    for b in range(4, levels):
        factors(b)

    scores = dot(query, key, ((1,), (1,)))
    scores_t = dot(key, query, ((1,), (1,)))
    sign = (1.0, -1.0)
    at = [sign[r] * t[r]["place"] for r in (0, 1)]
    frm = [sign[r] * t[r]["place"] - jnp.log(t[r]["soft"]) for r in (0, 1)]

    def three(v):
        parts = [p.astype(F32) for p in split3(v)]
        return jnp.concatenate(parts, axis=0).T.astype(BF16)

    at_cols = [three(v) for v in at]
    frm_cols = [three(v) for v in frm]
    rows_i, cols_i = iota((TOK, TOK), 0), iota((TOK, TOK), 1)
    lower, upper = rows_i >= cols_i, rows_i <= cols_i
    left = iota((TOK, LANES), 1) < LANES // 2
    ds_ref[...] = jnp.zeros_like(ds_ref)
    dk_ref[...] = jnp.zeros_like(dk_ref)
    dq_ref[...] = jnp.zeros_like(dq_ref)
    sums_ref[...] = jnp.zeros_like(sums_ref)
    head_row = iota((heads, TOK), 0)

    def row_of(v, h):
        return jnp.sum(jnp.where(head_row == h, v, 0.0), axis=0, keepdims=True)

    def inside(j, carry):
        lanes = pl.ds(pl.multiple_of(j * LANES, LANES), LANES)
        xb = x_ref[:, lanes]
        x = xb.astype(F32)
        g = g_ref[:, lanes].astype(F32) * mask
        zero = jnp.zeros_like(x)
        x_0, x_1 = jnp.where(left, x, zero).astype(BF16), jnp.where(left, zero, x).astype(BF16)
        g_0, g_1 = jnp.where(left, g, zero).astype(BF16), jnp.where(left, zero, g).astype(BF16)
        x_cat = jnp.concatenate([x_0, x_0, x_1, x_1], axis=0)
        g_cat = jnp.concatenate([g_0, g_0, g_1, g_1], axis=0)
        d_m = dot(jnp.concatenate([g_0, g_1], axis=0), xb, ((1,), (1,)))
        pick = iota((3 * heads, 2 * LANES), 0) % heads
        mine = 2 * j + (iota((3 * heads, 2 * LANES), 1) >= LANES).astype(jnp.int32)
        sel = jnp.where(pick == mine, 1.0, 0.0).astype(BF16)
        wsum = [0.0, 0.0]
        for r in (0, 1):
            at_b = dot(at_cols[r], sel)
            frm_b = dot(frm_cols[r], sel)
            m, m_t = [], []
            for k in (0, 1):
                at_row = row_of(at[r], 2 * j + k)
                frm_row = row_of(frm[r], 2 * j + k)
                cut = slice(k * LANES, (k + 1) * LANES)
                keep, keep_t = (lower, upper) if r == 0 else (upper, lower)
                wide = jnp.exp(jnp.where(keep, at_b[:, cut] - frm_row, -1e30))
                wide_t = jnp.exp(jnp.where(keep_t, at_row - frm_b[:, cut], -1e30))
                wsum[k] = wsum[k] + wide
                m += split2(wide * scores)
                m_t += split2(wide_t * scores_t)
            y_ref[r, j] = dot(jnp.concatenate(m, axis=1), x_cat)
            dx_ref[r, j] = dot(jnp.concatenate(m_t, axis=1), g_cat)
        ds_ref[...] += d_m[:TOK] * wsum[0] + d_m[TOK:] * wsum[1]
        return carry

    done = [0]

    def inside_some(count):
        stop = min(done[0] + count, tiles)
        if stop > done[0]:
            lax.fori_loop(done[0], stop, inside, 0)
        done[0] = stop

    def row(b, a, which, unit):
        return coef[b, a, which, pl.ds(unit // 2, 1), :]

    def joined(b, a, i):
        unit = base[b + 1] + i
        return row(b, a, 0, unit) * own[b][a, i] + row(b, a, 1, unit) * got[b][a, i].astype(F32)

    inside_some(PLAN[0])
    for b in range(1, levels):
        for a in range(4):
            up_copy(b - 1, a).wait_recv()

            def to_send(i, carry, b=b, a=a):
                snd[b][a, i] = joined(b - 1, a, (1 - bits[b]) * half[b] + i).astype(snd[b].dtype)
                return carry

            def to_keep(i, carry, b=b, a=a):
                own[b][a, i] = joined(b - 1, a, bits[b] * half[b] + i)
                return carry

            lax.fori_loop(0, half[b], to_send, 0, unroll=min(UNROLL, half[b]))
            up_copy(b, a).start()
            lax.fori_loop(0, half[b], to_keep, 0, unroll=min(UNROLL, half[b]))
        inside_some(PLAN[b])

    for b in range(levels - 1, -1, -1):
        if b == 0:
            inside_some(tiles)
        for a in range(4):
            late = late_flag(b, a)
            if b == levels - 1:
                up_copy(b, a).wait_recv()
            else:
                down_copy(b + 1, a).wait_recv()

            def entering(i, where, b=b, a=a):
                if where == "own":
                    return eown[b + 1][a, i]
                return egot[b + 1][a, i].astype(F32)

            def for_peer(i, at_unit, where, b=b, a=a, late=late):
                value = (1.0 - late) * own[b][a, at_unit]
                if where is not None:
                    value += row(b, a, 3, base[b + 1] + at_unit) * entering(i, where)
                esnd[b][a, at_unit] = value.astype(esnd[b].dtype)

            def for_me(i, at_unit, where, b=b, a=a, late=late):
                value = late * got[b][a, at_unit].astype(F32)
                if where is not None:
                    value += row(b, a, 2, base[b + 1] + at_unit) * entering(i, where)
                if b == 0:
                    hi, lo = split2(value)
                    e_hi[a, bits[0] * half[0] + at_unit] = hi
                    e_lo[a, bits[0] * half[0] + at_unit] = lo
                    e_lo[a, (1 - bits[0]) * half[0] + at_unit] = jnp.zeros_like(lo)
                else:
                    eown[b][a, at_unit] = value

            def sweep(fn, b=b):
                if b == levels - 1:
                    lax.fori_loop(0, half[b], lambda i, c: (fn(i, i, None), c)[1], 0)
                    return
                h = half[b + 1]
                n = min(UNROLL, h)
                mine, other = bits[b + 1] * h, (1 - bits[b + 1]) * h
                lax.fori_loop(0, h, lambda i, c: (fn(i, mine + i, "own"), c)[1], 0, unroll=n)
                lax.fori_loop(0, h, lambda i, c: (fn(i, other + i, "got"), c)[1], 0, unroll=n)

            sweep(for_peer)
            down_copy(b, a).start()
            sweep(for_me)

    skip2 = two_parts(jnp.broadcast_to(column(skip_ref[...]), (heads, TOK)))
    query2 = jnp.concatenate([query, query], axis=1)
    key2 = jnp.concatenate([key, key], axis=1)

    def carried(j):
        lanes = pl.ds(pl.multiple_of(j * LANES, LANES), LANES)
        x = x_ref[:, lanes].astype(F32)
        g = g_ref[:, lanes].astype(F32) * mask
        tile = pl.ds(2 * j, 2)

        def parts(a):
            hi = e_hi[a, tile].reshape(TOK, LANES)
            lo = e_lo[a, tile].reshape(TOK, LANES)
            return jnp.concatenate([hi, lo], axis=0), jnp.concatenate([hi, hi], axis=1), hi, lo

        enter = (parts(0), parts(2))
        back = (parts(3), parts(1))
        quant, y, dx = [], [], []
        for r in (0, 1):
            w_b, e_b = spread(w[r], j), spread(e[r], j)
            yr = y_ref[r, j] + e_b * dot(query2, enter[r][0])
            col_carried = w_b * dot(key2, back[r][0])
            dxr = dx_ref[r, j] + col_carried
            quant += [g * yr, x * dxr, x * col_carried]
            dk_ref[...] += dot(pair_lanes(x * w_b), back[r][1], ((1,), (1,)))
            dq_ref[...] += dot(pair_lanes(g * e_b), enter[r][1], ((1,), (1,)))
            through = (enter[r][2].astype(F32) + enter[r][3].astype(F32)) * (
                back[r][2].astype(F32) + back[r][3].astype(F32)
            )
            ge_ref[r, :, lanes] = jnp.sum(through.reshape(TOK // 8, 8, LANES), axis=0)
            y.append(yr)
            dx.append(dxr)
        quant.append(g * x)
        head_lane = 2 * j + (iota((heads, LANES), 1) >= LANES // 2).astype(jnp.int32)
        ones = jnp.where(iota((heads, LANES), 0) == head_lane, 1.0, 0.0).astype(BF16)
        ones2 = jnp.concatenate([ones, ones], axis=1)
        for n, q in enumerate(quant):
            sums_ref[n] += dot(ones2, pair_lanes(q), ((1,), (1,)))
        skip_b = spread(skip2, j)
        out_ref[:, lanes] = (mask * (y[0] + y[1] + skip_b * x)).astype(BF16)
        pg_ref[:, lanes] = (dx[0] + dx[1] + skip_b * g).astype(BF16)

    lax.fori_loop(0, half_tiles, lambda i, c: (carried(bits[0] * half_tiles + i), c)[1], 0)
    for a in range(4):
        down_copy(0, a).wait_recv()
    lax.fori_loop(0, half_tiles, lambda i, c: (carried((1 - bits[0]) * half_tiles + i), c)[1], 0)

    ds_hi, ds_lo = split2(ds_ref[...])
    qg_ref[...] = dq_ref[...] + dot(jnp.concatenate([ds_hi, ds_lo], axis=1), jnp.concatenate([key, key], axis=0))
    kg_ref[...] = (
        dk_ref[...] + dot(ds_hi, query, ((0,), (0,))) + dot(ds_lo, query, ((0,), (0,)))
    )

    width = tiles * LANES
    all_ones = jnp.where(
        iota((heads, width), 0) == iota((heads, width), 1) // (LANES // 2), 1.0, 0.0
    ).astype(BF16)
    upto = (rows_i <= cols_i).astype(F32)
    since = (rows_i >= cols_i).astype(F32)
    ones_row = jnp.ones((8, TOK), F32)

    def total_row(v):
        return dot(ones_row, v, ((1,), (1,)), precision=HIGH)[0:1]

    step_grad = jnp.zeros((heads, TOK), F32)
    decay_rows, bias_rows = [], []
    for r in (0, 1):
        hi, lo = split2(ge_ref[r])
        passing = jnp.sum(
            dot(all_ones, hi, ((1,), (1,))) + dot(all_ones, lo, ((1,), (1,))),
            axis=1, keepdims=True,
        )
        row_dot, col_dot, flow = sums_ref[3 * r], sums_ref[3 * r + 1], sums_ref[3 * r + 2]
        flow = jnp.exp(t[r]["total"]) * passing + jnp.sum(flow, axis=1, keepdims=True)
        d_log = flow + dot(row_dot - col_dot, since if r == 0 else upto, precision=HIGH)
        slope = t[r]["slope"] * mask
        raw_grad = col_dot * (slope / t[r]["soft"]) + t[r]["rate"] * d_log * slope
        step_grad += raw_grad
        decay_rows.append(-jnp.exp(logd[r : r + 1, :]) * total_row(t[r]["steps"] * d_log))
        bias_rows.append(total_row(raw_grad))
    sg_ref[...] = step_grad

    skip_row = total_row(sums_ref[6])
    value = jnp.concatenate(
        [
            jnp.concatenate(decay_rows + bias_rows, axis=1),
            jnp.concatenate([skip_row] * 4, axis=1),
        ],
        axis=0,
    )
    for n, part in enumerate((part_a, part_b, part_c)):
        place, size = sum_place[n], sum_size[n]
        part[place] = value
        for k in range(1, size):
            pltpu.make_async_remote_copy(
                src_ref=part.at[place], dst_ref=part.at[place],
                send_sem=sum_send.at[n, k], recv_sem=sum_recv.at[n, place],
                device_id=sum_peers[n][k - 1], device_id_type=MESH,
            ).start()
        for k in range(1, size):
            other = (place + k) % size
            pltpu.make_async_remote_copy(
                src_ref=part.at[other], dst_ref=part.at[other],
                send_sem=sum_send.at[n, k], recv_sem=sum_recv.at[n, other],
                device_id=sum_peers[n][k - 1], device_id_type=MESH,
            ).wait_recv()
        value = part[0]
        for k in range(1, size):
            value += part[k]
    for r in (0, 1):
        dec_ref[r : r + 1, :] = value[0:1, r * heads : (r + 1) * heads]
        bias_ref[r : r + 1, :] = value[0:1, (2 + r) * heads : (3 + r) * heads]
    skipg_ref[...] = value[1:2, :heads]

    for b in range(levels):
        log_copy(b).wait_send()
        for a in range(4):
            up_copy(b, a).wait_send()
            down_copy(b, a).wait_send()
    for n, part in enumerate((part_a, part_b, part_c)):
        for k in range(1, sum_size[n]):
            pltpu.make_async_remote_copy(
                src_ref=part.at[sum_place[n]], dst_ref=part.at[sum_place[n]],
                send_sem=sum_send.at[n, k], recv_sem=sum_recv.at[n, sum_place[n]],
                device_id=sum_peers[n][k - 1], device_id_type=MESH,
            ).wait_send()


def body(
    patches, key_proj, query_proj, step_raw, log_decay, step_bias, skip_gain, group_valid, out_grad
):
    heads = step_raw.shape[1]
    width = patches.shape[2]
    tiles = width // LANES
    units = 2 * tiles
    seq = lax.axis_size("seq")
    groups = lax.axis_size("dp")
    levels = seq.bit_length() - 1
    line = min(8, seq)
    rows_of = seq // line
    vmem = pl.BlockSpec(memory_space=pltpu.VMEM)
    h = [units >> (b + 1) for b in range(levels)]
    unit = (TOK // 2, LANES)
    link = [LINK[b] for b in range(levels)]

    def blocks(dtypes):
        return [pltpu.VMEM((4, h[b]) + unit, dtypes[b]) for b in range(levels)]

    wide = [F32] * levels
    dma = pltpu.SemaphoreType.DMA
    size = max(line, rows_of, groups)
    output, patch_grad, key_grad, query_grad, step_grad, decay_grad, bias_grad, skip_grad = (
        pl.pallas_call(
            functools.partial(
                layer_kernel, levels=levels, units=units, tiles=tiles,
                line=line, rows_of=rows_of, groups=groups,
            ),
            out_shape=(
                jax.ShapeDtypeStruct((TOK, width), BF16),
                jax.ShapeDtypeStruct((TOK, width), BF16),
                jax.ShapeDtypeStruct((TOK, LANES), F32),
                jax.ShapeDtypeStruct((TOK, LANES), F32),
                jax.ShapeDtypeStruct((heads, TOK), F32),
                jax.ShapeDtypeStruct((2, heads), F32),
                jax.ShapeDtypeStruct((2, heads), F32),
                jax.ShapeDtypeStruct((1, heads), F32),
            ),
            in_specs=[vmem] * 8 + [pl.BlockSpec(memory_space=pltpu.SMEM)],
            out_specs=(vmem,) * 8,
            scratch_shapes=[
                pltpu.VMEM((levels, 2, tiles, LANES), F32),
                pltpu.VMEM((levels, 2, tiles, LANES), F32),
                pltpu.VMEM((levels, 4, 4, tiles, LANES), F32),
                blocks(wide),
                blocks(link),
                blocks(link),
                blocks(wide),
                blocks(link),
                blocks(link),
                pltpu.VMEM((4, units) + unit, BF16),
                pltpu.VMEM((4, units) + unit, BF16),
                pltpu.VMEM((2, tiles, TOK, LANES), F32),
                pltpu.VMEM((2, tiles, TOK, LANES), F32),
                pltpu.VMEM((2, 8, width), F32),
                pltpu.VMEM((TOK, TOK), F32),
                pltpu.VMEM((TOK, LANES), F32),
                pltpu.VMEM((TOK, LANES), F32),
                pltpu.VMEM((7, heads, TOK), F32),
                pltpu.VMEM((line, 2, LANES), F32),
                pltpu.VMEM((rows_of, 2, LANES), F32),
                pltpu.VMEM((groups, 2, LANES), F32),
                dma((levels, 4)),
                dma((levels, 4)),
                dma((levels, 4)),
                dma((levels, 4)),
                dma((levels,)),
                dma((levels,)),
                dma((3, size)),
                dma((3, size)),
            ],
            compiler_params=pltpu.CompilerParams(collective_id=0, has_side_effects=True),
            name="layer",
        )(
            patches[0], out_grad[0], key_proj[0], query_proj[0], step_raw[0],
            log_decay, step_bias, skip_gain[None], group_valid,
        )
    )
    return (
        output[None],
        patch_grad[None],
        key_grad[None],
        query_grad[None],
        step_grad[None],
        decay_grad,
        bias_grad,
        skip_grad[0],
    )


def solution(mesh):
    in_specs = (
        P("dp", "seq", None),
        P("dp", "seq", None),
        P("dp", "seq", None),
        P("dp", None, "seq"),
        P(),
        P(),
        P(),
        P("dp", "seq"),
        P("dp", "seq", None),
    )
    out_specs = (
        P("dp", "seq", None),
        P("dp", "seq", None),
        P("dp", "seq", None),
        P("dp", "seq", None),
        P("dp", None, "seq"),
        P(),
        P(),
        P(),
    )
    return jax.shard_map(body, mesh=mesh, in_specs=in_specs, out_specs=out_specs, check_vma=False)
```

```python
import functools

import jax
import jax.numpy as jnp
from jax import lax
from jax.experimental import pallas as pl
from jax.experimental.pallas import tpu as pltpu
from jax.sharding import PartitionSpec as P

F32 = jnp.float32
BF16 = jnp.bfloat16
MESH = pl.DeviceIdType.MESH
TOK = 128
LANES = 128
HIGH = lax.Precision.HIGHEST

SCAN_DIR = (0, 1, 1, 0)
SCAN_LEFT = (False, False, True, True)


def dot(a, b, dims=((1,), (0,)), precision=None):
    return lax.dot_general(
        a, b, (dims, ((), ())), precision=precision, preferred_element_type=F32
    )


def iota(shape, axis):
    return lax.broadcasted_iota(jnp.int32, shape, axis)


def split2(v):
    hi = v.astype(BF16)
    return hi, (v - hi.astype(F32)).astype(BF16)


def split3(v):
    hi = v.astype(BF16)
    rest = v - hi.astype(F32)
    mid = rest.astype(BF16)
    return hi, mid, (rest - mid.astype(F32)).astype(BF16)


def column(row):
    heads = row.shape[1]
    eye = iota((heads, heads), 0) == iota((heads, heads), 1)
    return jnp.sum(jnp.where(eye, jnp.broadcast_to(row, (heads, heads)), 0.0), axis=1, keepdims=True)


def softplus(v):
    z = jnp.exp(-jnp.abs(v))
    u = z / (2.0 + z)
    q = u * u
    series = 1.0 / 17.0
    for term in (15.0, 13.0, 11.0, 9.0, 7.0, 5.0, 3.0, 1.0):
        series = series * q + 1.0 / term
    return jnp.maximum(v, 0.0) + 2.0 * u * series


def timing(raw, log_decay, step_bias, mask, r):
    rate = -jnp.exp(column(log_decay[r : r + 1, :]))
    shifted = raw + column(step_bias[r : r + 1, :])
    soft = softplus(shifted)
    slope = 1.0 / (1.0 + jnp.exp(-shifted))
    steps = soft * mask
    logs = steps * rate
    upto = (iota((TOK, TOK), 0) <= iota((TOK, TOK), 1)).astype(F32)
    cum = dot(logs, upto, precision=HIGH)
    total = cum[:, TOK - 1 :]
    if r == 0:
        place = cum
        weight = jnp.exp(total - cum) * steps
        decay = jnp.exp(cum)
    else:
        place = cum - logs
        weight = jnp.exp(place) * steps
        decay = jnp.exp(total - place)
    return dict(
        rate=rate, soft=soft, slope=slope, steps=steps, total=total, place=place,
        weight=weight, decay=decay,
    )


def spread(pair, tile):
    rows = pair.shape[1]
    pick = iota((rows, LANES), 0) % (rows // 2)
    mine = 2 * tile + (iota((rows, LANES), 1) >= LANES // 2).astype(jnp.int32)
    return dot(pair, jnp.where(pick == mine, 1.0, 0.0).astype(BF16))


def parts_t(parts):
    return jnp.concatenate([p.astype(F32) for p in parts], axis=0).T.astype(BF16)


ARRAYS = 4
SPLIT = 2
PIECES = ARRAYS * SPLIT
ROWS = 32
PER_TILE = TOK // ROWS
LINK = (BF16, BF16, BF16, F32, F32)
MOVE = ({"core": 3.2}, {"outer": 13.5}, {"outer": 6.8, "inner": 13.5}, {"x": 6.8}, {"x": 6.8})
WAIT = (1.0, 1.7, 2.4, 1.7, 2.4)
STATES_US, STEPS_US, INSIDE_US, CARRIED_US = 6.5, 2.0, 0.65, 0.5


def step_order(levels, tiles):
    free = {}
    clock = 0.0
    order, waiting, ready_tiles = [], [], []
    inside = 0
    landed = [0] * SPLIT
    share = tiles // SPLIT

    def send(level, kind, piece):
        end = clock
        for link, us in MOVE[level].items():
            free[link] = max(clock, free.get(link, 0.0)) + us / PIECES
            end = max(end, free[link])
        waiting.append((end + WAIT[level], len(order), kind, level, piece))

    def one_inside():
        nonlocal inside, clock
        order.append(("inside", 0, inside))
        inside += 1
        clock += INSIDE_US

    def one_carried():
        nonlocal clock
        tile = ready_tiles.pop(0)
        while inside <= tile:
            one_inside()
        order.append(("carried", 0, tile))
        clock += CARRIED_US

    for q in range(SPLIT):
        for a in range(ARRAYS):
            piece = SPLIT * a + q
            clock += STATES_US / PIECES / 2
            order.append(("state", 0, piece))
            send(0, "up", piece)
            clock += STATES_US / PIECES / 2
    while waiting:
        waiting.sort()
        ready = waiting[0][0]
        if ready_tiles and ready > clock + CARRIED_US:
            one_carried()
            continue
        if inside < tiles and ready > clock + INSIDE_US:
            one_inside()
            continue
        _, _, kind, level, piece = waiting.pop(0)
        if kind == "down" and level == 0:
            q = piece % SPLIT
            landed[q] += 1
            if landed[q] == ARRAYS:
                order.append(("landed", 0, q))
                ready_tiles.extend(range(q * share, (q + 1) * share))
            continue
        clock = max(clock, ready) + STEPS_US / PIECES
        if kind == "up" and level + 1 < levels:
            order.append(("up", level + 1, piece))
            send(level + 1, "up", piece)
        else:
            below = level if kind == "up" else level - 1
            order.append(("down", below, piece))
            send(below, "down", piece)
    while ready_tiles:
        one_carried()
    return order


def pair_rows(v):
    hi, lo = split2(v)
    return jnp.concatenate([hi, lo], axis=0)


def pair_lanes(v):
    hi, lo = split2(v)
    return jnp.concatenate([hi, lo], axis=1)


def layer_kernel(
    x_ref, g_ref, key_ref, query_ref, raw_ref, ld_ref, sb_ref, skip_ref, valid_ref,
    out_ref, pg_ref, kg_ref, qg_ref, sg_ref, val_ref,
    seg, seg_in, coef, own, got, snd, eown, egot, esnd, e_hi, e_lo,
    y_ref, dx_ref, ge_ref, ds_ref, dk_ref, dq_ref, sums_ref, part_a, part_b, part_c,
    up_send, up_recv, down_send, down_recv, log_send, log_recv,
    sum_send, sum_recv, *, levels, units, tiles, line, rows_of, groups
):
    me = lax.axis_index("seq")
    my_dp = lax.axis_index("dp")
    bits = [(me // (1 << b)) % 2 for b in range(levels)]
    peers = [me + (1 << b) * (1 - 2 * bits[b]) for b in range(levels)]
    half = [units >> (b + 1) for b in range(levels)]
    base = [0]
    for b in range(levels):
        base.append(base[b] + bits[b] * half[b])

    in_line = me % line
    my_line = me // line
    sum_peers = (
        [{"seq": my_line * line + (in_line + k) % line} for k in range(1, line)],
        [{"seq": (my_line + k) % rows_of * line + in_line} for k in range(1, rows_of)],
        [{"dp": (my_dp + k) % groups} for k in range(1, groups)],
    )
    sum_place = (in_line, my_line, my_dp)
    sum_size = (line, rows_of, groups)

    barrier = pltpu.get_barrier_semaphore()
    greeted = 0
    for group in sum_peers:
        for device in group:
            pl.semaphore_signal(barrier, inc=1, device_id=device, device_id_type=MESH)
            greeted += 1

    mask = valid_ref[0, 0].astype(F32)
    raw = raw_ref[...]
    logd = ld_ref[...]
    bias = sb_ref[...]
    heads = raw.shape[0]
    t = [timing(raw, logd, bias, mask, r) for r in (0, 1)]
    pick = iota((tiles, heads), 1)
    even = (pick == 2 * iota((tiles, heads), 0)).astype(F32)
    odd = (pick == 2 * iota((tiles, heads), 0) + 1).astype(F32)
    left_row = iota((tiles, LANES), 1) < LANES // 2
    for r in (0, 1):
        wide = jnp.broadcast_to(t[r]["total"], (heads, LANES))
        seg[0, r] = jnp.where(
            left_row, dot(even, wide, precision=HIGH), dot(odd, wide, precision=HIGH)
        )
    w = [parts_t(split2(t[r]["weight"])) for r in (0, 1)]
    e = [parts_t(split2(t[r]["decay"])) for r in (0, 1)]
    key = key_ref[...]
    query = query_ref[...]

    pl.semaphore_wait(barrier, greeted)

    def push(src, dst, send, recv, b):
        return pltpu.make_async_remote_copy(
            src_ref=src, dst_ref=dst, send_sem=send, recv_sem=recv,
            device_id={"seq": peers[b]}, device_id_type=MESH,
        )

    def up_copy(b, a):
        return push(snd[b].at[a], got[b].at[a], up_send.at[b, a], up_recv.at[b, a], b)

    def down_copy(b, a):
        if b == 0:
            dst = e_hi.at[a, pl.ds(bits[0] * half[0], half[0])]
        else:
            dst = egot[b].at[a]
        return push(esnd[b].at[a], dst, down_send.at[b, a], down_recv.at[b, a], b)

    def log_copy(b):
        return push(seg.at[b], seg_in.at[b], log_send.at[b], log_recv.at[b], b)

    def late_flag(b, a):
        late = (1 - bits[b]) if SCAN_LEFT[a] else bits[b]
        return late.astype(F32)

    def factors(b):
        log_copy(b).wait_recv()
        mine, other = seg[b], seg_in[b]
        if b + 2 < levels:
            seg[b + 1] = mine + other
            log_copy(b + 1).start()
        for a in range(ARRAYS):
            r = SCAN_DIR[a]
            late = late_flag(b, a)
            coef[b, a, 0] = jnp.exp((1.0 - late) * other[r])
            coef[b, a, 1] = jnp.exp(late * mine[r])
            coef[b, a, 2] = jnp.exp(late * other[r])
            coef[b, a, 3] = jnp.exp((1.0 - late) * mine[r])

    log_copy(0).start()

    key_t = key.astype(F32).T.astype(BF16)
    query_t = query.astype(F32).T.astype(BF16)
    key_tt = jnp.concatenate([key_t, key_t], axis=1)
    query_tt = jnp.concatenate([query_t, query_t], axis=1)
    half_tiles = tiles // 2
    piece_tiles = tiles // SPLIT
    keep_tiles = piece_tiles // 2
    scale = (w[0], e[1], w[1], e[0])

    def states(piece):
        a, q = piece // SPLIT, piece % SPLIT
        is_state = a % 2 == 0
        ref, lhs = (x_ref, key_tt) if is_state else (g_ref, query_tt)

        def state(at_tile):
            j = q * piece_tiles + at_tile
            lanes = pl.ds(pl.multiple_of(j * LANES, LANES), LANES)
            v = ref[:, lanes].astype(F32) * spread(scale[a], j)
            if not is_state:
                v = v * mask
            return dot(lhs, pair_rows(v)).reshape(PER_TILE, ROWS, LANES)

        def state_out(i, carry):
            u = state((1 - bits[0]) * keep_tiles + i)
            snd[0][piece, pl.ds(PER_TILE * i, PER_TILE)] = u.astype(snd[0].dtype)
            return carry

        def state_keep(i, carry):
            own[0][piece, pl.ds(PER_TILE * i, PER_TILE)] = state(bits[0] * keep_tiles + i)
            return carry

        lax.fori_loop(0, keep_tiles, state_out, 0, unroll=True)
        up_copy(0, piece).start()
        lax.fori_loop(0, keep_tiles, state_keep, 0, unroll=True)

    scores = dot(query, key, ((1,), (1,)))
    scores_t = dot(key, query, ((1,), (1,)))
    sign = (1.0, -1.0)
    at = [sign[r] * t[r]["place"] for r in (0, 1)]
    frm = [sign[r] * t[r]["place"] - jnp.log(t[r]["soft"]) for r in (0, 1)]

    at_cols = [parts_t(split3(v)) for v in at]
    frm_cols = [parts_t(split3(v)) for v in frm]
    rows_i, cols_i = iota((TOK, TOK), 0), iota((TOK, TOK), 1)
    lower, upper = rows_i >= cols_i, rows_i <= cols_i
    left = iota((TOK, LANES), 1) < LANES // 2
    ds_ref[...] = jnp.zeros_like(ds_ref)
    dk_ref[...] = jnp.zeros_like(dk_ref)
    dq_ref[...] = jnp.zeros_like(dq_ref)
    sums_ref[...] = jnp.zeros_like(sums_ref)
    head_row = iota((heads, TOK), 0)

    def row_of(v, h):
        return jnp.sum(jnp.where(head_row == h, v, 0.0), axis=0, keepdims=True)

    def head_ones(j):
        head = 2 * j + (iota((heads, LANES), 1) >= LANES // 2).astype(jnp.int32)
        return jnp.where(iota((heads, LANES), 0) == head, 1.0, 0.0).astype(BF16)

    def inside(j):
        lanes = pl.ds(pl.multiple_of(j * LANES, LANES), LANES)
        xb = x_ref[:, lanes]
        x = xb.astype(F32)
        g = g_ref[:, lanes].astype(F32) * mask
        zero = jnp.zeros_like(x)
        x_0, x_1 = jnp.where(left, x, zero).astype(BF16), jnp.where(left, zero, x).astype(BF16)
        g_0, g_1 = jnp.where(left, g, zero).astype(BF16), jnp.where(left, zero, g).astype(BF16)
        x_cat = jnp.concatenate([x_0, x_0, x_1, x_1], axis=0)
        g_cat = jnp.concatenate([g_0, g_0, g_1, g_1], axis=0)
        d_m = dot(jnp.concatenate([g_0, g_1], axis=0), xb, ((1,), (1,)))
        pick = iota((3 * heads, 2 * LANES), 0) % heads
        mine = 2 * j + (iota((3 * heads, 2 * LANES), 1) >= LANES).astype(jnp.int32)
        sel = jnp.where(pick == mine, 1.0, 0.0).astype(BF16)
        wsum = [0.0, 0.0]
        y, dx = [], []
        for r in (0, 1):
            at_b = dot(at_cols[r], sel)
            frm_b = dot(frm_cols[r], sel)
            m, m_t = [], []
            for k in (0, 1):
                at_row = row_of(at[r], 2 * j + k)
                frm_row = row_of(frm[r], 2 * j + k)
                cut = slice(k * LANES, (k + 1) * LANES)
                keep, keep_t = (lower, upper) if r == 0 else (upper, lower)
                wide = jnp.exp(jnp.where(keep, at_b[:, cut] - frm_row, -1e30))
                wide_t = jnp.exp(jnp.where(keep_t, at_row - frm_b[:, cut], -1e30))
                wsum[k] = wsum[k] + wide
                m += split2(wide * scores)
                m_t += split2(wide_t * scores_t)
            y.append(dot(jnp.concatenate(m, axis=1), x_cat))
            dx.append(dot(jnp.concatenate(m_t, axis=1), g_cat))
        ds_ref[...] += d_m[:TOK] * wsum[0] + d_m[TOK:] * wsum[1]
        y_ref[j] = y[0] + y[1]
        dx_ref[j] = dx[0] + dx[1]
        ones = head_ones(j)
        ones2 = jnp.concatenate([ones, ones], axis=1)
        quant = [x * dx[0], g * y[0] - x * dx[0], x * dx[1], g * y[1] - x * dx[1], g * x]
        for n, q in enumerate(quant):
            sums_ref[n] += dot(ones2, pair_lanes(q), ((1,), (1,)))

    def factor(b, a, which, unit):
        tile = (a % SPLIT) * piece_tiles + unit // PER_TILE
        return coef[b, a // SPLIT, which, pl.ds(tile, 1), :].reshape(1, 1, LANES)

    def each(count, most, fn):
        size = min(PER_TILE, most, count)
        if count == size:
            fn(0, size)
        else:
            lax.fori_loop(0, count // size, lambda i, c: (fn(i * size, size), c)[1], 0, unroll=2)

    def join(b, a):
        up_copy(b - 1, a).wait_recv()

        def joined(first, size):
            unit = base[b] + first
            mine = own[b - 1][a, pl.ds(first, size)]
            other = got[b - 1][a, pl.ds(first, size)].astype(F32)
            return factor(b - 1, a, 0, unit) * mine + factor(b - 1, a, 1, unit) * other

        def to_send(first, size):
            value = joined((1 - bits[b]) * half[b] + first, size)
            snd[b][a, pl.ds(first, size)] = value.astype(snd[b].dtype)

        def to_keep(first, size):
            own[b][a, pl.ds(first, size)] = joined(bits[b] * half[b] + first, size)

        each(half[b], PER_TILE, to_send)
        up_copy(b, a).start()
        each(half[b], PER_TILE, to_keep)

    def enter_down(b, a):
        late = late_flag(b, a // SPLIT)
        top = b == levels - 1
        if top:
            up_copy(b, a).wait_recv()
        else:
            down_copy(b + 1, a).wait_recv()

        def entering(first, size, where):
            if where == "own":
                return eown[b + 1][a, pl.ds(first, size)]
            return egot[b + 1][a, pl.ds(first, size)].astype(F32)

        def for_peer(first, size, at_unit, where):
            value = (1.0 - late) * own[b][a, pl.ds(at_unit, size)]
            if where is not None:
                value += factor(b, a, 3, base[b + 1] + at_unit) * entering(first, size, where)
            esnd[b][a, pl.ds(at_unit, size)] = value.astype(esnd[b].dtype)

        def for_me(first, size, at_unit, where):
            value = late * got[b][a, pl.ds(at_unit, size)].astype(F32)
            if where is not None:
                value += factor(b, a, 2, base[b + 1] + at_unit) * entering(first, size, where)
            if b == 0:
                hi, lo = split2(value)
                e_hi[a, pl.ds(bits[0] * half[0] + at_unit, size)] = hi
                e_lo[a, pl.ds(bits[0] * half[0] + at_unit, size)] = lo
                e_lo[a, pl.ds((1 - bits[0]) * half[0] + at_unit, size)] = jnp.zeros_like(lo)
            else:
                eown[b][a, pl.ds(at_unit, size)] = value

        def sweep(fn):
            if top:
                each(half[b], PER_TILE, lambda first, size: fn(first, size, first, None))
                return
            h = half[b + 1]
            for where, start in (("own", bits[b + 1] * h), ("got", (1 - bits[b + 1]) * h)):
                each(h, PER_TILE, lambda f, n, where=where, start=start: fn(f, n, start + f, where))

        sweep(for_peer)
        down_copy(b, a).start()
        sweep(for_me)

    skip2 = parts_t(split2(jnp.broadcast_to(column(skip_ref[...]), (heads, TOK))))
    query2 = jnp.concatenate([query, query], axis=1)
    key2 = jnp.concatenate([key, key], axis=1)

    def entered(a, j):
        piece = SPLIT * a + j // piece_tiles
        tile = pl.ds(PER_TILE * (j % piece_tiles), PER_TILE)
        return e_hi[piece, tile].reshape(TOK, LANES), e_lo[piece, tile].reshape(TOK, LANES)

    def carried(j):
        lanes = pl.ds(pl.multiple_of(j * LANES, LANES), LANES)
        x = x_ref[:, lanes].astype(F32)
        g = g_ref[:, lanes].astype(F32) * mask
        ones = head_ones(j)
        ones2 = jnp.concatenate([ones, ones], axis=1)
        y, dx = y_ref[j], dx_ref[j]
        for r, (a_in, a_back) in enumerate(((0, 3), (2, 1))):
            e_in, e_back = entered(a_in, j), entered(a_back, j)
            y_more = spread(e[r], j) * dot(query2, jnp.concatenate(e_in, axis=0))
            dx_more = spread(w[r], j) * dot(key2, jnp.concatenate(e_back, axis=0))
            sums_ref[5 + 2 * r] += dot(ones2, pair_lanes(g * y_more), ((1,), (1,)))
            sums_ref[6 + 2 * r] += dot(ones2, pair_lanes(x * dx_more), ((1,), (1,)))
            through = (e_in[0].astype(F32) + e_in[1].astype(F32)) * (
                e_back[0].astype(F32) + e_back[1].astype(F32)
            )
            ge_ref[r, :, lanes] = jnp.sum(through.reshape(TOK // 8, 8, LANES), axis=0)
            y, dx = y + y_more, dx + dx_more
        skip_b = spread(skip2, j)
        out_ref[:, lanes] = (mask * (y + skip_b * x)).astype(BF16)
        pg_ref[:, lanes] = (dx + skip_b * g).astype(BF16)

    factored, made = 0, 0
    for kind, level, n in step_order(levels, tiles):
        if kind == "state":
            states(n)
            made += 1
            if made % SPLIT == 0 and factored < levels - 1:
                factors(factored)
                factored += 1
        elif kind == "up":
            while factored < min(level + 1, levels - 1):
                factors(factored)
                factored += 1
            join(level, n)
        elif kind == "down":
            while factored < levels - 1:
                factors(factored)
                factored += 1
            enter_down(level, n)
        elif kind == "landed":
            for a in range(ARRAYS):
                down_copy(0, SPLIT * a + n).wait_recv()
        elif kind == "inside":
            inside(n)
        else:
            carried(n)

    def projections(j):
        lanes = pl.ds(pl.multiple_of(j * LANES, LANES), LANES)
        x = x_ref[:, lanes].astype(F32)
        g = g_ref[:, lanes].astype(F32) * mask
        left_sides, right_sides = ([], []), ([], [])
        for r, (a_in, a_back) in enumerate(((0, 3), (2, 1))):
            hi, _ = entered(a_back, j)
            left_sides[0].append(pair_lanes(x * spread(w[r], j)))
            right_sides[0].extend([hi, hi])
            hi, _ = entered(a_in, j)
            left_sides[1].append(pair_lanes(g * spread(e[r], j)))
            right_sides[1].extend([hi, hi])
        for n, acc in enumerate((dk_ref, dq_ref)):
            acc[...] += dot(
                jnp.concatenate(left_sides[n], axis=1),
                jnp.concatenate(right_sides[n], axis=1),
                ((1,), (1,)),
            )

    projected = [0]

    def project_some(stop):
        if stop > projected[0]:
            lax.fori_loop(projected[0], stop, lambda i, c: (projections(i), c)[1], 0)
        projected[0] = stop

    width = tiles * LANES
    all_ones = jnp.where(
        iota((heads, width), 0) == iota((heads, width), 1) // (LANES // 2), 1.0, 0.0
    ).astype(BF16)
    upto = (rows_i <= cols_i).astype(F32)
    since = (rows_i >= cols_i).astype(F32)
    ones_row = jnp.ones((8, TOK), F32)

    def total_row(v):
        return dot(ones_row, v, ((1,), (1,)), precision=HIGH)[0:1]

    step_grad = jnp.zeros((heads, TOK), F32)
    decay_rows, bias_rows = [], []
    for r in (0, 1):
        hi, lo = split2(ge_ref[r])
        passing = jnp.sum(
            dot(all_ones, hi, ((1,), (1,))) + dot(all_ones, lo, ((1,), (1,))),
            axis=1, keepdims=True,
        )
        col_in, net_in = sums_ref[2 * r], sums_ref[2 * r + 1]
        row_more, col_more = sums_ref[5 + 2 * r], sums_ref[6 + 2 * r]
        flow = jnp.exp(t[r]["total"]) * passing + jnp.sum(col_more, axis=1, keepdims=True)
        net = net_in + row_more - col_more
        d_log = flow + dot(net, since if r == 0 else upto, precision=HIGH)
        slope = t[r]["slope"] * mask
        raw_grad = (col_in + col_more) * (slope / t[r]["soft"]) + t[r]["rate"] * d_log * slope
        step_grad += raw_grad
        decay_rows.append(-jnp.exp(logd[r : r + 1, :]) * total_row(t[r]["steps"] * d_log))
        bias_rows.append(total_row(raw_grad))
    sg_ref[...] = step_grad

    skip_row = total_row(sums_ref[4])
    value = jnp.concatenate(
        [
            jnp.concatenate(decay_rows + bias_rows, axis=1),
            jnp.concatenate([skip_row] * 4, axis=1),
        ],
        axis=0,
    )
    for n, part in enumerate((part_a, part_b, part_c)):
        place, size = sum_place[n], sum_size[n]
        part[place] = value
        for k in range(1, size):
            pltpu.make_async_remote_copy(
                src_ref=part.at[place], dst_ref=part.at[place],
                send_sem=sum_send.at[n, k], recv_sem=sum_recv.at[n, place],
                device_id=sum_peers[n][k - 1], device_id_type=MESH,
            ).start()
        project_some((tiles // 3, 2 * tiles // 3, tiles)[n])
        for k in range(1, size):
            other = (place + k) % size
            pltpu.make_async_remote_copy(
                src_ref=part.at[other], dst_ref=part.at[other],
                send_sem=sum_send.at[n, k], recv_sem=sum_recv.at[n, other],
                device_id=sum_peers[n][k - 1], device_id_type=MESH,
            ).wait_recv()
        value = part[0]
        for k in range(1, size):
            value += part[k]
    ds_hi, ds_lo = split2(ds_ref[...])
    qg_ref[...] = dq_ref[...] + dot(
        jnp.concatenate([ds_hi, ds_lo], axis=1), jnp.concatenate([key, key], axis=0)
    )
    kg_ref[...] = (
        dk_ref[...] + dot(ds_hi, query, ((0,), (0,))) + dot(ds_lo, query, ((0,), (0,)))
    )
    val_ref[...] = value

    for b in range(levels):
        if b + 1 < levels:
            log_copy(b).wait_send()
        for a in range(PIECES):
            up_copy(b, a).wait_send()
            down_copy(b, a).wait_send()
    for n, part in enumerate((part_a, part_b, part_c)):
        for k in range(1, sum_size[n]):
            pltpu.make_async_remote_copy(
                src_ref=part.at[sum_place[n]], dst_ref=part.at[sum_place[n]],
                send_sem=sum_send.at[n, k], recv_sem=sum_recv.at[n, sum_place[n]],
                device_id=sum_peers[n][k - 1], device_id_type=MESH,
            ).wait_send()


def finish_kernel(*refs):
    for source, target in zip(refs[:5], refs[6:11]):
        target[...] = source[...]
    value = refs[5][...]
    dec_ref, bias_ref, skipg_ref = refs[11:]
    heads = dec_ref.shape[1]
    for r in (0, 1):
        dec_ref[r : r + 1, :] = value[0:1, r * heads : (r + 1) * heads]
        bias_ref[r : r + 1, :] = value[0:1, (2 + r) * heads : (3 + r) * heads]
    skipg_ref[...] = value[1:2, :heads]


def body(
    patches, key_proj, query_proj, step_raw, log_decay, step_bias, skip_gain, group_valid, out_grad
):
    heads = step_raw.shape[1]
    width = patches.shape[2]
    tiles = width // LANES
    units = tiles // SPLIT * PER_TILE
    seq = lax.axis_size("seq")
    groups = lax.axis_size("dp")
    levels = seq.bit_length() - 1
    line = min(8, seq)
    rows_of = seq // line
    vmem = pl.BlockSpec(memory_space=pltpu.VMEM)
    h = [units >> (b + 1) for b in range(levels)]
    unit = (ROWS, LANES)
    link = [LINK[b] for b in range(levels)]

    def blocks(dtypes):
        return [pltpu.VMEM((PIECES, h[b]) + unit, dtypes[b]) for b in range(levels)]

    wide = [F32] * levels
    dma = pltpu.SemaphoreType.DMA
    size = max(line, rows_of, groups)
    made = (
        pl.pallas_call(
            functools.partial(
                layer_kernel, levels=levels, units=units, tiles=tiles,
                line=line, rows_of=rows_of, groups=groups,
            ),
            out_shape=(
                jax.ShapeDtypeStruct((TOK, width), BF16),
                jax.ShapeDtypeStruct((TOK, width), BF16),
                jax.ShapeDtypeStruct((TOK, LANES), F32),
                jax.ShapeDtypeStruct((TOK, LANES), F32),
                jax.ShapeDtypeStruct((heads, TOK), F32),
                jax.ShapeDtypeStruct((2, LANES), F32),
            ),
            in_specs=[vmem] * 8 + [pl.BlockSpec(memory_space=pltpu.SMEM)],
            out_specs=(vmem,) * 6,
            scratch_shapes=[
                pltpu.VMEM((levels, 2, tiles, LANES), F32),
                pltpu.VMEM((levels, 2, tiles, LANES), F32),
                pltpu.VMEM((levels, 4, 4, tiles, LANES), F32),
                blocks(wide),
                blocks(link),
                blocks(link),
                blocks(wide),
                blocks(link),
                blocks(link),
                pltpu.VMEM((PIECES, units) + unit, BF16),
                pltpu.VMEM((PIECES, units) + unit, BF16),
                pltpu.VMEM((tiles, TOK, LANES), F32),
                pltpu.VMEM((tiles, TOK, LANES), F32),
                pltpu.VMEM((2, 8, width), F32),
                pltpu.VMEM((TOK, TOK), F32),
                pltpu.VMEM((TOK, LANES), F32),
                pltpu.VMEM((TOK, LANES), F32),
                pltpu.VMEM((9, heads, TOK), F32),
                pltpu.VMEM((line, 2, LANES), F32),
                pltpu.VMEM((rows_of, 2, LANES), F32),
                pltpu.VMEM((groups, 2, LANES), F32),
                dma((levels, PIECES)),
                dma((levels, PIECES)),
                dma((levels, PIECES)),
                dma((levels, PIECES)),
                dma((levels,)),
                dma((levels,)),
                dma((3, size)),
                dma((3, size)),
            ],
            compiler_params=pltpu.CompilerParams(collective_id=0, has_side_effects=True),
            name="layer",
        )(
            patches[0], out_grad[0], key_proj[0], query_proj[0], step_raw[0],
            log_decay, step_bias, skip_gain[None], group_valid,
        )
    )
    output, patch_grad, key_grad, query_grad, step_grad, decay_grad, bias_grad, skip_grad = (
        pl.pallas_call(
            finish_kernel,
            out_shape=tuple(jax.ShapeDtypeStruct(m.shape, m.dtype) for m in made[:5])
            + (
                jax.ShapeDtypeStruct((2, heads), F32),
                jax.ShapeDtypeStruct((2, heads), F32),
                jax.ShapeDtypeStruct((1, heads), F32),
            ),
            in_specs=[vmem] * 6,
            out_specs=(vmem,) * 8,
            name="finish",
        )(*made)
    )
    return (
        output[None],
        patch_grad[None],
        key_grad[None],
        query_grad[None],
        step_grad[None],
        decay_grad,
        bias_grad,
        skip_grad[0],
    )


def solution(mesh):
    in_specs = (
        P("dp", "seq", None),
        P("dp", "seq", None),
        P("dp", "seq", None),
        P("dp", None, "seq"),
        P(),
        P(),
        P(),
        P("dp", "seq"),
        P("dp", "seq", None),
    )
    out_specs = (
        P("dp", "seq", None),
        P("dp", "seq", None),
        P("dp", "seq", None),
        P("dp", "seq", None),
        P("dp", None, "seq"),
        P(),
        P(),
        P(),
    )
    return jax.shard_map(body, mesh=mesh, in_specs=in_specs, out_specs=out_specs, check_vma=False)
```

```python
import functools

import jax
import jax.numpy as jnp
from jax import lax
from jax.experimental import pallas as pl
from jax.experimental.pallas import tpu as pltpu
from jax.sharding import PartitionSpec as P

F32 = jnp.float32
BF16 = jnp.bfloat16
MESH = pl.DeviceIdType.MESH
TOK = 128
LANES = 128

SCAN_DIR = (0, 1, 1, 0)
SCAN_LEFT = (False, False, True, True)


def dot(a, b, dims=((1,), (0,))):
    return lax.dot_general(a, b, (dims, ((), ())), preferred_element_type=F32)


def iota(shape, axis):
    return lax.broadcasted_iota(jnp.int32, shape, axis)


def split2(v):
    hi = v.astype(BF16)
    return hi, (v - hi.astype(F32)).astype(BF16)


def split3(v):
    hi = v.astype(BF16)
    rest = v - hi.astype(F32)
    mid = rest.astype(BF16)
    return hi, mid, (rest - mid.astype(F32)).astype(BF16)


def column(row):
    heads = row.shape[1]
    eye = iota((heads, heads), 0) == iota((heads, heads), 1)
    return jnp.sum(jnp.where(eye, jnp.broadcast_to(row, (heads, heads)), 0.0), axis=1, keepdims=True)


def softplus(v):
    z = jnp.exp(-jnp.abs(v))
    u = z / (2.0 + z)
    q = u * u
    series = 1.0 / 17.0
    for term in (15.0, 13.0, 11.0, 9.0, 7.0, 5.0, 3.0, 1.0):
        series = series * q + 1.0 / term
    return jnp.maximum(v, 0.0) + 2.0 * u * series


def timing(raw, log_decay, step_bias, mask, r):
    rate = -jnp.exp(column(log_decay[r : r + 1, :]))
    shifted = raw + column(step_bias[r : r + 1, :])
    soft = softplus(shifted)
    slope = 1.0 / (1.0 + jnp.exp(-shifted))
    steps = soft * mask
    logs = steps * rate
    upto = (iota((TOK, TOK), 0) <= iota((TOK, TOK), 1)).astype(F32).astype(BF16)
    cum = dot(jnp.concatenate(split3(logs), axis=1), jnp.concatenate([upto] * 3, axis=0))
    total = cum[:, TOK - 1 :]
    if r == 0:
        place = cum
        weight = jnp.exp(total - cum) * steps
        decay = jnp.exp(cum)
    else:
        place = cum - logs
        weight = jnp.exp(place) * steps
        decay = jnp.exp(total - place)
    return dict(
        rate=rate, soft=soft, slope=slope, steps=steps, total=total, place=place,
        weight=weight, decay=decay,
    )


def spread(pair, tile):
    rows = pair.shape[1]
    pick = iota((rows, LANES), 0) % (rows // 2)
    mine = 2 * tile + (iota((rows, LANES), 1) >= LANES // 2).astype(jnp.int32)
    return dot(pair, jnp.where(pick == mine, 1.0, 0.0).astype(BF16))


def parts_t(parts):
    return jnp.concatenate([p.astype(F32) for p in parts], axis=0).T.astype(BF16)


ARRAYS = 4
SPLIT = 2
PIECES = ARRAYS * SPLIT
ROWS = 32
PER_TILE = TOK // ROWS
LINK = (BF16, BF16, BF16, F32, F32)
MOVE = ({"core": 2.5}, {"outer": 10.5}, {"outer": 5.2, "inner": 10.5}, {"x": 5.0}, {"x": 5.0})
WAIT = (1.5, 3.0, 4.0, 3.0, 4.0)
STATES_US, STEPS_US, INSIDE_US, CARRIED_US = 6.5, 2.0, 0.65, 0.5


def step_order(levels, tiles):
    free = {}
    clock = 0.0
    order, waiting, ready_tiles = [], [], []
    inside = 0
    sent, landed = [0] * SPLIT, [0] * SPLIT
    share = tiles // SPLIT
    states = [SPLIT * a + q for q in range(SPLIT) for a in range(ARRAYS)]

    def send(level, kind, piece):
        end = clock
        for link, us in MOVE[level].items():
            free[link] = max(clock, free.get(link, 0.0)) + us / PIECES
            end = max(end, free[link])
        waiting.append((end + WAIT[level], len(order), kind, level, piece))

    def one_inside():
        nonlocal inside, clock
        order.append(("inside", 0, inside))
        inside += 1
        clock += INSIDE_US

    def one_carried():
        nonlocal clock
        kind, q, i = ready_tiles.pop(0)
        while inside < (q + 1) * share:
            one_inside()
        order.append((kind, q, i))
        clock += CARRIED_US

    while waiting or states:
        waiting.sort()
        ready = waiting[0][0] if waiting else float("inf")
        if states and ready > clock:
            piece = states.pop(0)
            clock += STATES_US / PIECES / 2
            order.append(("state", 0, piece))
            send(0, "up", piece)
            clock += STATES_US / PIECES / 2
            continue
        if ready_tiles and ready > clock + CARRIED_US:
            one_carried()
            continue
        if inside < tiles and ready > clock + INSIDE_US:
            one_inside()
            continue
        _, _, kind, level, piece = waiting.pop(0)
        if kind == "down" and level == 0:
            q = piece % SPLIT
            landed[q] += 1
            if landed[q] == ARRAYS:
                order.append(("landed", q, q))
                ready_tiles.extend(("other", q, i) for i in range(share // 2))
            continue
        clock = max(clock, ready) + STEPS_US / PIECES
        if kind == "up" and level + 1 < levels:
            order.append(("up", level + 1, piece))
            send(level + 1, "up", piece)
        else:
            below = level if kind == "up" else level - 1
            order.append(("down", below, piece))
            send(below, "down", piece)
            if below == 0:
                q = piece % SPLIT
                sent[q] += 1
                if sent[q] == ARRAYS:
                    ready_tiles.extend(("own", q, i) for i in range(share // 2))
    while ready_tiles:
        one_carried()
    return order


def pair_rows(v):
    hi, lo = split2(v)
    return jnp.concatenate([hi, lo], axis=0)


def pair_lanes(v):
    hi, lo = split2(v)
    return jnp.concatenate([hi, lo], axis=1)


def layer_kernel(
    x_hbm, g_hbm, key_ref, query_ref, raw_ref, ld_ref, sb_ref, skip_ref, valid_ref,
    out_hbm, pg_hbm, kg_ref, qg_ref, sg_ref, val_ref,
    x_ref, g_ref, out_ref, pg_ref, seg, seg_in, coef, own, got, snd, eown, egot, esnd, e_hi, e_lo,
    y_ref, dx_ref, ge_ref, ds_ref, dk_ref, dq_ref, sums_ref, part_a, part_b, part_c,
    up_send, up_recv, down_send, down_recv, log_send, log_recv,
    sum_send, sum_recv, load_sem, store_sem, *, levels, units, tiles, line, rows_of, groups
):
    me = lax.axis_index("seq")
    my_dp = lax.axis_index("dp")
    bits = [(me // (1 << b)) % 2 for b in range(levels)]
    peers = [me + (1 << b) * (1 - 2 * bits[b]) for b in range(levels)]
    half = [units >> (b + 1) for b in range(levels)]
    base = [0]
    for b in range(levels):
        base.append(base[b] + bits[b] * half[b])

    in_line = me % line
    my_line = me // line
    sum_peers = (
        [{"seq": my_line * line + (in_line + k) % line} for k in range(1, line)],
        [{"seq": (my_line + k) % rows_of * line + in_line} for k in range(1, rows_of)],
        [{"dp": (my_dp + k) % groups} for k in range(1, groups)],
    )
    sum_place = (in_line, my_line, my_dp)
    sum_size = (line, rows_of, groups)

    loads = [
        pltpu.make_async_copy(x_hbm, x_ref, load_sem.at[0]),
        pltpu.make_async_copy(g_hbm, g_ref, load_sem.at[1]),
    ]
    for load in loads:
        load.start()

    barrier = pltpu.get_barrier_semaphore()
    greeted = 0
    for group in sum_peers:
        for device in group:
            pl.semaphore_signal(barrier, inc=1, device_id=device, device_id_type=MESH)
            greeted += 1

    mask = valid_ref[0, 0].astype(F32)
    raw = raw_ref[...]
    logd = ld_ref[...]
    bias = sb_ref[...]
    heads = raw.shape[0]
    t = [timing(raw, logd, bias, mask, r) for r in (0, 1)]
    pick_row = iota((2 * tiles, 3 * heads), 0)
    pick_head = jnp.where(pick_row < tiles, 2 * pick_row, 2 * (pick_row - tiles) + 1)
    picks = iota((2 * tiles, 3 * heads), 1) % heads == pick_head
    picks = jnp.where(picks, 1.0, 0.0).astype(BF16)
    left_row = iota((tiles, LANES), 1) < LANES // 2
    for r in (0, 1):
        parts = [p.astype(F32) for p in split3(jnp.broadcast_to(t[r]["total"], (heads, LANES)))]
        rows = dot(picks, jnp.concatenate(parts, axis=0).astype(BF16))
        seg[0, r] = jnp.where(left_row, rows[:tiles], rows[tiles:])
    w = [parts_t(split2(t[r]["weight"])) for r in (0, 1)]
    e = [parts_t(split2(t[r]["decay"])) for r in (0, 1)]
    key = key_ref[...]
    query = query_ref[...]

    pl.semaphore_wait(barrier, greeted)

    def push(src, dst, send, recv, b):
        return pltpu.make_async_remote_copy(
            src_ref=src, dst_ref=dst, send_sem=send, recv_sem=recv,
            device_id={"seq": peers[b]}, device_id_type=MESH,
        )

    def up_copy(b, a):
        return push(snd[b].at[a], got[b].at[a], up_send.at[b, a], up_recv.at[b, a], b)

    def down_copy(b, a):
        if b == 0:
            dst = e_hi.at[a, pl.ds(bits[0] * half[0], half[0])]
        else:
            dst = egot[b].at[a]
        return push(esnd[b].at[a], dst, down_send.at[b, a], down_recv.at[b, a], b)

    def log_copy(b):
        return push(seg.at[b], seg_in.at[b], log_send.at[b], log_recv.at[b], b)

    def late_flag(b, a):
        late = (1 - bits[b]) if SCAN_LEFT[a] else bits[b]
        return late.astype(F32)

    def factors(b):
        log_copy(b).wait_recv()
        mine, other = seg[b], seg_in[b]
        if b + 2 < levels:
            seg[b + 1] = mine + other
            log_copy(b + 1).start()
        for a in range(ARRAYS):
            r = SCAN_DIR[a]
            late = late_flag(b, a)
            coef[b, a, 0] = jnp.exp((1.0 - late) * other[r])
            coef[b, a, 1] = jnp.exp(late * mine[r])
            coef[b, a, 2] = jnp.exp(late * other[r])
            coef[b, a, 3] = jnp.exp((1.0 - late) * mine[r])

    log_copy(0).start()
    for load in loads:
        load.wait()

    key_t = key.astype(F32).T.astype(BF16)
    query_t = query.astype(F32).T.astype(BF16)
    key_tt = jnp.concatenate([key_t, key_t], axis=1)
    query_tt = jnp.concatenate([query_t, query_t], axis=1)
    half_tiles = tiles // 2
    piece_tiles = tiles // SPLIT
    keep_tiles = piece_tiles // 2
    scale = (w[0], e[1], w[1], e[0])

    def states(piece):
        a, q = piece // SPLIT, piece % SPLIT
        is_state = a % 2 == 0
        ref, lhs = (x_ref, key_tt) if is_state else (g_ref, query_tt)

        def state(at_tile):
            j = q * piece_tiles + at_tile
            lanes = pl.ds(pl.multiple_of(j * LANES, LANES), LANES)
            v = ref[:, lanes].astype(F32) * spread(scale[a], j)
            if not is_state:
                v = v * mask
            return dot(lhs, pair_rows(v)).reshape(PER_TILE, ROWS, LANES)

        def state_out(i, carry):
            u = state((1 - bits[0]) * keep_tiles + i)
            snd[0][piece, pl.ds(PER_TILE * i, PER_TILE)] = u.astype(snd[0].dtype)
            return carry

        def state_keep(i, carry):
            own[0][piece, pl.ds(PER_TILE * i, PER_TILE)] = state(bits[0] * keep_tiles + i)
            return carry

        lax.fori_loop(0, keep_tiles, state_out, 0, unroll=True)
        up_copy(0, piece).start()
        lax.fori_loop(0, keep_tiles, state_keep, 0, unroll=True)

    scores = dot(query, key, ((1,), (1,)))
    scores_t = dot(key, query, ((1,), (1,)))
    sign = (1.0, -1.0)
    at = [sign[r] * t[r]["place"] for r in (0, 1)]
    frm = [sign[r] * t[r]["place"] - jnp.log(t[r]["soft"]) for r in (0, 1)]

    at_cols = [parts_t(split3(v)) for v in at]
    frm_cols = [parts_t(split3(v)) for v in frm]
    rows_i, cols_i = iota((TOK, TOK), 0), iota((TOK, TOK), 1)
    lower, upper = rows_i >= cols_i, rows_i <= cols_i
    left = iota((TOK, LANES), 1) < LANES // 2
    ds_ref[...] = jnp.zeros_like(ds_ref)
    dk_ref[...] = jnp.zeros_like(dk_ref)
    dq_ref[...] = jnp.zeros_like(dq_ref)
    sums_ref[...] = jnp.zeros_like(sums_ref)
    ge_ref[...] = jnp.zeros_like(ge_ref)
    head_row = iota((heads, TOK), 0)

    def row_of(v, h):
        return jnp.sum(jnp.where(head_row == h, v, 0.0), axis=0, keepdims=True)

    def head_ones(j):
        head = 2 * j + (iota((heads, LANES), 1) >= LANES // 2).astype(jnp.int32)
        return jnp.where(iota((heads, LANES), 0) == head, 1.0, 0.0).astype(BF16)

    def inside(j):
        lanes = pl.ds(pl.multiple_of(j * LANES, LANES), LANES)
        xb = x_ref[:, lanes]
        x = xb.astype(F32)
        g = g_ref[:, lanes].astype(F32) * mask
        zero = jnp.zeros_like(x)
        x_0, x_1 = jnp.where(left, x, zero).astype(BF16), jnp.where(left, zero, x).astype(BF16)
        g_0, g_1 = jnp.where(left, g, zero).astype(BF16), jnp.where(left, zero, g).astype(BF16)
        x_cat = jnp.concatenate([x_0, x_0, x_1, x_1], axis=0)
        g_cat = jnp.concatenate([g_0, g_0, g_1, g_1], axis=0)
        d_m = dot(jnp.concatenate([g_0, g_1], axis=0), xb, ((1,), (1,)))
        pick = iota((3 * heads, 2 * LANES), 0) % heads
        mine = 2 * j + (iota((3 * heads, 2 * LANES), 1) >= LANES).astype(jnp.int32)
        sel = jnp.where(pick == mine, 1.0, 0.0).astype(BF16)
        wsum = [0.0, 0.0]
        y, dx = [], []
        for r in (0, 1):
            at_b = dot(at_cols[r], sel)
            frm_b = dot(frm_cols[r], sel)
            m, m_t = [], []
            for k in (0, 1):
                at_row = row_of(at[r], 2 * j + k)
                frm_row = row_of(frm[r], 2 * j + k)
                cut = slice(k * LANES, (k + 1) * LANES)
                keep, keep_t = (lower, upper) if r == 0 else (upper, lower)
                wide = jnp.exp(jnp.where(keep, at_b[:, cut] - frm_row, -1e30))
                wide_t = jnp.exp(jnp.where(keep_t, at_row - frm_b[:, cut], -1e30))
                wsum[k] = wsum[k] + wide
                m += split2(wide * scores)
                m_t += split2(wide_t * scores_t)
            y.append(dot(jnp.concatenate(m, axis=1), x_cat))
            dx.append(dot(jnp.concatenate(m_t, axis=1), g_cat))
        ds_ref[...] += d_m[:TOK] * wsum[0] + d_m[TOK:] * wsum[1]
        y_ref[j] = y[0] + y[1]
        dx_ref[j] = dx[0] + dx[1]
        ones = head_ones(j)
        ones2 = jnp.concatenate([ones, ones], axis=1)
        quant = [x * dx[0], g * y[0] - x * dx[0], x * dx[1], g * y[1] - x * dx[1], g * x]
        for n, q in enumerate(quant):
            sums_ref[n] += dot(ones2, pair_lanes(q), ((1,), (1,)))

    def factor(b, a, which, unit):
        tile = (a % SPLIT) * piece_tiles + unit // PER_TILE
        return coef[b, a // SPLIT, which, pl.ds(tile, 1), :].reshape(1, 1, LANES)

    def each(count, most, fn):
        size = min(PER_TILE, most, count)
        if count == size:
            fn(0, size)
        else:
            lax.fori_loop(0, count // size, lambda i, c: (fn(i * size, size), c)[1], 0, unroll=2)

    def join(b, a):
        up_copy(b - 1, a).wait_recv()

        def joined(first, size):
            unit = base[b] + first
            mine = own[b - 1][a, pl.ds(first, size)]
            other = got[b - 1][a, pl.ds(first, size)].astype(F32)
            return factor(b - 1, a, 0, unit) * mine + factor(b - 1, a, 1, unit) * other

        def to_send(first, size):
            value = joined((1 - bits[b]) * half[b] + first, size)
            snd[b][a, pl.ds(first, size)] = value.astype(snd[b].dtype)

        def to_keep(first, size):
            own[b][a, pl.ds(first, size)] = joined(bits[b] * half[b] + first, size)

        each(half[b], PER_TILE, to_send)
        up_copy(b, a).start()
        each(half[b], PER_TILE, to_keep)

    def enter_down(b, a):
        late = late_flag(b, a // SPLIT)
        top = b == levels - 1
        if top:
            up_copy(b, a).wait_recv()
        else:
            down_copy(b + 1, a).wait_recv()

        def entering(first, size, where):
            if where == "own":
                return eown[b + 1][a, pl.ds(first, size)]
            return egot[b + 1][a, pl.ds(first, size)].astype(F32)

        def for_peer(first, size, at_unit, where):
            value = (1.0 - late) * own[b][a, pl.ds(at_unit, size)]
            if where is not None:
                value += factor(b, a, 3, base[b + 1] + at_unit) * entering(first, size, where)
            esnd[b][a, pl.ds(at_unit, size)] = value.astype(esnd[b].dtype)

        def for_me(first, size, at_unit, where):
            value = late * got[b][a, pl.ds(at_unit, size)].astype(F32)
            if where is not None:
                value += factor(b, a, 2, base[b + 1] + at_unit) * entering(first, size, where)
            if b == 0:
                hi, lo = split2(value)
                e_hi[a, pl.ds(bits[0] * half[0] + at_unit, size)] = hi
                e_lo[a, pl.ds(bits[0] * half[0] + at_unit, size)] = lo
                e_lo[a, pl.ds((1 - bits[0]) * half[0] + at_unit, size)] = jnp.zeros_like(lo)
            else:
                eown[b][a, pl.ds(at_unit, size)] = value

        def sweep(fn):
            if top:
                each(half[b], PER_TILE, lambda first, size: fn(first, size, first, None))
                return
            h = half[b + 1]
            for where, start in (("own", bits[b + 1] * h), ("got", (1 - bits[b + 1]) * h)):
                each(h, PER_TILE, lambda f, n, where=where, start=start: fn(f, n, start + f, where))

        sweep(for_peer)
        down_copy(b, a).start()
        sweep(for_me)

    skip2 = parts_t(split2(jnp.broadcast_to(column(skip_ref[...]), (heads, TOK))))
    query2 = jnp.concatenate([query, query], axis=1)
    key2 = jnp.concatenate([key, key], axis=1)

    def entered(a, j):
        piece = SPLIT * a + j // piece_tiles
        tile = pl.ds(PER_TILE * (j % piece_tiles), PER_TILE)
        return e_hi[piece, tile].reshape(TOK, LANES), e_lo[piece, tile].reshape(TOK, LANES)

    def carried(j):
        lanes = pl.ds(pl.multiple_of(j * LANES, LANES), LANES)
        x = x_ref[:, lanes].astype(F32)
        g = g_ref[:, lanes].astype(F32) * mask
        ones = head_ones(j)
        ones2 = jnp.concatenate([ones, ones], axis=1)
        y, dx = y_ref[j], dx_ref[j]
        for r, (a_in, a_back) in enumerate(((0, 3), (2, 1))):
            e_in, e_back = entered(a_in, j), entered(a_back, j)
            y_more = spread(e[r], j) * dot(query2, jnp.concatenate(e_in, axis=0))
            dx_more = spread(w[r], j) * dot(key2, jnp.concatenate(e_back, axis=0))
            sums_ref[5 + 2 * r] += dot(ones2, pair_lanes(g * y_more), ((1,), (1,)))
            sums_ref[6 + 2 * r] += dot(ones2, pair_lanes(x * dx_more), ((1,), (1,)))
            through = (e_in[0].astype(F32) + e_in[1].astype(F32)) * (
                e_back[0].astype(F32) + e_back[1].astype(F32)
            )
            through = jnp.sum(through.reshape(TOK // 8, 8, LANES), axis=0)
            ge_ref[r] += dot(ones2, pair_lanes(through), ((1,), (1,)))
            y, dx = y + y_more, dx + dx_more
        y_ref[j] = y
        dx_ref[j] = dx

    factored, made = 0, 0
    for kind, level, n in step_order(levels, tiles):
        if kind == "state":
            states(n)
            made += 1
            if made % SPLIT == 0 and factored < levels - 1:
                factors(factored)
                factored += 1
        elif kind == "up":
            while factored < min(level + 1, levels - 1):
                factors(factored)
                factored += 1
            join(level, n)
        elif kind == "down":
            while factored < levels - 1:
                factors(factored)
                factored += 1
            enter_down(level, n)
        elif kind == "landed":
            for a in range(ARRAYS):
                down_copy(0, SPLIT * a + n).wait_recv()
        elif kind == "inside":
            inside(n)
        else:
            bit = bits[0] if kind == "own" else 1 - bits[0]
            carried(level * piece_tiles + bit * keep_tiles + n)

    def projections(j):
        lanes = pl.ds(pl.multiple_of(j * LANES, LANES), LANES)
        x = x_ref[:, lanes].astype(F32)
        g = g_ref[:, lanes].astype(F32) * mask
        skip_b = spread(skip2, j)
        out_ref[:, lanes] = (mask * (y_ref[j] + skip_b * x)).astype(BF16)
        pg_ref[:, lanes] = (dx_ref[j] + skip_b * g).astype(BF16)
        left_sides, right_sides = ([], []), ([], [])
        for r, (a_in, a_back) in enumerate(((0, 3), (2, 1))):
            hi, _ = entered(a_back, j)
            left_sides[0].append(pair_lanes(x * spread(w[r], j)))
            right_sides[0].extend([hi, hi])
            hi, _ = entered(a_in, j)
            left_sides[1].append(pair_lanes(g * spread(e[r], j)))
            right_sides[1].extend([hi, hi])
        for n, acc in enumerate((dk_ref, dq_ref)):
            acc[...] += dot(
                jnp.concatenate(left_sides[n], axis=1),
                jnp.concatenate(right_sides[n], axis=1),
                ((1,), (1,)),
            )

    stores = [
        pltpu.make_async_copy(out_ref, out_hbm, store_sem.at[0]),
        pltpu.make_async_copy(pg_ref, pg_hbm, store_sem.at[1]),
    ]
    projected = [0]

    def project_some(stop):
        if stop > projected[0]:
            lax.fori_loop(projected[0], stop, lambda i, c: (projections(i), c)[1], 0)
        projected[0] = stop

    upto = jnp.where(rows_i <= cols_i, 1.0, 0.0).astype(BF16)
    since = jnp.where(rows_i >= cols_i, 1.0, 0.0).astype(BF16)
    step_grad = jnp.zeros((heads, TOK), F32)
    rates = [-jnp.exp(logd[r : r + 1, :]) for r in (0, 1)]
    by_decay, by_bias = [], []
    for r in (0, 1):
        passing = jnp.sum(ge_ref[r], axis=1, keepdims=True)
        col_in, net_in = sums_ref[2 * r], sums_ref[2 * r + 1]
        row_more, col_more = sums_ref[5 + 2 * r], sums_ref[6 + 2 * r]
        flow = jnp.exp(t[r]["total"]) * passing + jnp.sum(col_more, axis=1, keepdims=True)
        net = net_in + row_more - col_more
        over = since if r == 0 else upto
        d_log = flow + dot(pair_lanes(net), jnp.concatenate([over, over], axis=0))
        slope = t[r]["slope"] * mask
        raw_grad = (col_in + col_more) * (slope / t[r]["soft"]) + t[r]["rate"] * d_log * slope
        step_grad += raw_grad
        by_decay.append(t[r]["steps"] * d_log)
        by_bias.append(raw_grad)
    sg_ref[...] = step_grad

    summed = jnp.concatenate(by_decay + by_bias + [sums_ref[4]], axis=0)
    totals = dot(jnp.ones((8, 2 * TOK), BF16), pair_lanes(summed), ((1,), (1,)))[0:1]
    value = jnp.concatenate(
        [
            jnp.concatenate(
                [rates[0] * totals[:, :heads], rates[1] * totals[:, heads : 2 * heads],
                 totals[:, 2 * heads : 4 * heads]], axis=1,
            ),
            jnp.concatenate([totals[:, 4 * heads :]] * 4, axis=1),
        ],
        axis=0,
    )
    for n, part in enumerate((part_a, part_b, part_c)):
        place, size = sum_place[n], sum_size[n]
        part[place] = value
        for k in range(1, size):
            pltpu.make_async_remote_copy(
                src_ref=part.at[place], dst_ref=part.at[place],
                send_sem=sum_send.at[n, k], recv_sem=sum_recv.at[n, place],
                device_id=sum_peers[n][k - 1], device_id_type=MESH,
            ).start()
        project_some((tiles // 2, tiles, tiles)[n])
        if n == 1:
            for store in stores:
                store.start()
        for k in range(1, size):
            other = (place + k) % size
            pltpu.make_async_remote_copy(
                src_ref=part.at[other], dst_ref=part.at[other],
                send_sem=sum_send.at[n, k], recv_sem=sum_recv.at[n, other],
                device_id=sum_peers[n][k - 1], device_id_type=MESH,
            ).wait_recv()
        value = part[0]
        for k in range(1, size):
            value += part[k]
    ds_hi, ds_lo = split2(ds_ref[...])
    qg_ref[...] = dq_ref[...] + dot(
        jnp.concatenate([ds_hi, ds_lo], axis=1), jnp.concatenate([key, key], axis=0)
    )
    kg_ref[...] = (
        dk_ref[...] + dot(ds_hi, query, ((0,), (0,))) + dot(ds_lo, query, ((0,), (0,)))
    )
    val_ref[...] = value
    for store in stores:
        store.wait()

    for b in range(levels):
        if b + 1 < levels:
            log_copy(b).wait_send()
        for a in range(PIECES):
            up_copy(b, a).wait_send()
            down_copy(b, a).wait_send()
    for n, part in enumerate((part_a, part_b, part_c)):
        for k in range(1, sum_size[n]):
            pltpu.make_async_remote_copy(
                src_ref=part.at[sum_place[n]], dst_ref=part.at[sum_place[n]],
                send_sem=sum_send.at[n, k], recv_sem=sum_recv.at[n, sum_place[n]],
                device_id=sum_peers[n][k - 1], device_id_type=MESH,
            ).wait_send()


def finish_kernel(*refs):
    for source, target in zip(refs[:5], refs[6:11]):
        target[...] = source[...]
    value = refs[5][...]
    dec_ref, bias_ref, skipg_ref = refs[11:]
    heads = dec_ref.shape[1]
    for r in (0, 1):
        dec_ref[r : r + 1, :] = value[0:1, r * heads : (r + 1) * heads]
        bias_ref[r : r + 1, :] = value[0:1, (2 + r) * heads : (3 + r) * heads]
    skipg_ref[...] = value[1:2, :heads]


def body(
    patches, key_proj, query_proj, step_raw, log_decay, step_bias, skip_gain, group_valid, out_grad
):
    heads = step_raw.shape[1]
    width = patches.shape[2]
    tiles = width // LANES
    units = tiles // SPLIT * PER_TILE
    seq = lax.axis_size("seq")
    groups = lax.axis_size("dp")
    levels = seq.bit_length() - 1
    line = min(8, seq)
    rows_of = seq // line
    vmem = pl.BlockSpec(memory_space=pltpu.VMEM)
    h = [units >> (b + 1) for b in range(levels)]
    unit = (ROWS, LANES)
    link = [LINK[b] for b in range(levels)]

    def blocks(dtypes):
        return [pltpu.VMEM((PIECES, h[b]) + unit, dtypes[b]) for b in range(levels)]

    wide = [F32] * levels
    dma = pltpu.SemaphoreType.DMA
    size = max(line, rows_of, groups)
    made = (
        pl.pallas_call(
            functools.partial(
                layer_kernel, levels=levels, units=units, tiles=tiles,
                line=line, rows_of=rows_of, groups=groups,
            ),
            out_shape=(
                jax.ShapeDtypeStruct((TOK, width), BF16),
                jax.ShapeDtypeStruct((TOK, width), BF16),
                jax.ShapeDtypeStruct((TOK, LANES), F32),
                jax.ShapeDtypeStruct((TOK, LANES), F32),
                jax.ShapeDtypeStruct((heads, TOK), F32),
                jax.ShapeDtypeStruct((2, LANES), F32),
            ),
            in_specs=[pl.BlockSpec(memory_space=pl.ANY)] * 2 + [vmem] * 6 + [pl.BlockSpec(memory_space=pltpu.SMEM)],
            out_specs=(pl.BlockSpec(memory_space=pl.ANY),) * 2 + (vmem,) * 4,
            scratch_shapes=[
                pltpu.VMEM((TOK, width), BF16),
                pltpu.VMEM((TOK, width), BF16),
                pltpu.VMEM((TOK, width), BF16),
                pltpu.VMEM((TOK, width), BF16),
                pltpu.VMEM((levels, 2, tiles, LANES), F32),
                pltpu.VMEM((levels, 2, tiles, LANES), F32),
                pltpu.VMEM((levels, 4, 4, tiles, LANES), F32),
                blocks(wide),
                blocks(link),
                blocks(link),
                blocks(wide),
                blocks(link),
                blocks(link),
                pltpu.VMEM((PIECES, units) + unit, BF16),
                pltpu.VMEM((PIECES, units) + unit, BF16),
                pltpu.VMEM((tiles, TOK, LANES), F32),
                pltpu.VMEM((tiles, TOK, LANES), F32),
                pltpu.VMEM((2, heads, 8), F32),
                pltpu.VMEM((TOK, TOK), F32),
                pltpu.VMEM((TOK, LANES), F32),
                pltpu.VMEM((TOK, LANES), F32),
                pltpu.VMEM((9, heads, TOK), F32),
                pltpu.VMEM((line, 2, LANES), F32),
                pltpu.VMEM((rows_of, 2, LANES), F32),
                pltpu.VMEM((groups, 2, LANES), F32),
                dma((levels, PIECES)),
                dma((levels, PIECES)),
                dma((levels, PIECES)),
                dma((levels, PIECES)),
                dma((levels,)),
                dma((levels,)),
                dma((3, size)),
                dma((3, size)),
                dma((2,)),
                dma((2,)),
            ],
            compiler_params=pltpu.CompilerParams(collective_id=0, has_side_effects=True),
            name="layer",
        )(
            patches[0], out_grad[0], key_proj[0], query_proj[0], step_raw[0],
            log_decay, step_bias, skip_gain[None], group_valid,
        )
    )
    output, patch_grad, key_grad, query_grad, step_grad, decay_grad, bias_grad, skip_grad = (
        pl.pallas_call(
            finish_kernel,
            out_shape=tuple(jax.ShapeDtypeStruct(m.shape, m.dtype) for m in made[:5])
            + (
                jax.ShapeDtypeStruct((2, heads), F32),
                jax.ShapeDtypeStruct((2, heads), F32),
                jax.ShapeDtypeStruct((1, heads), F32),
            ),
            in_specs=[vmem] * 6,
            out_specs=(vmem,) * 8,
            name="finish",
        )(*made)
    )
    return (
        output[None],
        patch_grad[None],
        key_grad[None],
        query_grad[None],
        step_grad[None],
        decay_grad,
        bias_grad,
        skip_grad[0],
    )


def solution(mesh):
    in_specs = (
        P("dp", "seq", None),
        P("dp", "seq", None),
        P("dp", "seq", None),
        P("dp", None, "seq"),
        P(),
        P(),
        P(),
        P("dp", "seq"),
        P("dp", "seq", None),
    )
    out_specs = (
        P("dp", "seq", None),
        P("dp", "seq", None),
        P("dp", "seq", None),
        P("dp", "seq", None),
        P("dp", None, "seq"),
        P(),
        P(),
        P(),
    )
    return jax.shard_map(body, mesh=mesh, in_specs=in_specs, out_specs=out_specs, check_vma=False)
```
